32 devices in a mesh: crop: 2 (over y), rows: 4 (over x, core), hid: 4 (over z).
Axes of the slice: x: 2, y: 2, z: 4, core: 2. Of those that a mesh axis runs over, the one named last changes fastest.
Arguments:
- tokens: bfloat16 [2, 8, 64, 4096], P('crop', 'rows', None, 'hid'), may hold values from -6 to 6
- cotangent: bfloat16 [2, 8, 64, 4096], P('crop', 'rows', None, 'hid'), may hold values from -6 to 6
- weight_in: bfloat16 [256, 64, 5, 256], P('rows', 'hid'), may hold values from -0.15625 to 0.15625
- weight_out: bfloat16 [256, 64, 5, 256], P('rows', 'hid'), may hold values from -0.078125 to 0.078125
- mix_kernel: float32 [9, 16384], P(None, 'hid'), may hold values from -4 to 4
- block_rows: int32 [64, 5], P('hid'), may hold values from 0 to 15, as said below
Outputs:
- grad_tokens: bfloat16 [2, 8, 64, 4096], P('crop', 'rows', None, 'hid')
- grad_w_in: float32 [256, 64, 5, 256], P(('crop', 'rows'), 'hid')
- grad_w_out: float32 [256, 64, 5, 256], P(('crop', 'rows'), 'hid')
- grad_kernel: float32 [9, 16384], P(None, 'hid')
The draws below stay inside these ranges and needn't reach their ends.
Inputs may be any that keep to these rules, and one draw needn't show every extreme that they name: In each block column c, block_rows[c, 0] is a label L and block_rows[c, k] for k >= 1 is L with bit k - 1 flipped, so the 5 entries of a column differ; every value is the label of equally many block columns.
All inputs are finite; a program needn't handle non-finite values.
Results may differ from the reference program's by a relative error of at most 0.019.
Values may be sent and summed in bfloat16 or wider, within the bound.
A program may use at most 128 MiB of HBM per device.

```python
import jax
import jax.numpy as jnp
from jax import lax

D = 4096
F = 16384
BS = 256
NNZ = 5
PW = 64
CROPS = 2
GH = 8
FB = 64
N_ROWS = 4


def draw_block_rows(key, part):
    block_count = D // BS
    perm_key, flip_key = jax.random.split(jax.random.fold_in(key, 7))
    labels = jax.random.permutation(perm_key, jnp.arange(F // BS, dtype=jnp.int32)) % block_count
    flip_bits = jax.random.randint(flip_key, (), 0, block_count).astype(jnp.int32)
    labels = jnp.bitwise_xor(labels, flip_bits)
    shifts = jnp.left_shift(jnp.ones((NNZ - 1,), jnp.int32), jnp.arange(NNZ - 1, dtype=jnp.int32))
    masks = jnp.concatenate([jnp.zeros((1,), jnp.int32), shifts])
    return jnp.bitwise_xor(labels[:, None], masks[None, :]).astype(jnp.int32)


def steps_of(own_key, dims, shards, low, largest):
    gain, own = 1.0, jax.random.fold_in(own_key, 6)
    for axis_at, shards_of in shards:
        steps = jnp.exp(jax.random.uniform(jax.random.fold_in(own, axis_at), (shards_of,), jnp.float32, low / len(shards), largest / len(shards)))
        gain = gain * jnp.repeat(steps, dims[axis_at] // shards_of).reshape([-1 if axis == axis_at else 1 for axis in range(len(dims))])
    return gain


def noise(own_key, shape, width, bound, cuts=(), held_as=jnp.bfloat16):
    entries = width * jax.random.normal(own_key, shape, jnp.float32)
    if cuts:
        entries = entries * steps_of(own_key, shape, cuts, -0.22, 0.18)
    return jnp.clip(entries, -bound, bound).astype(held_as)


def setup_inputs(seed: int = 0) -> dict:
    splits = jax.random.split(jax.random.key(seed), 7)
    tokens = noise(splits[0], (CROPS, GH, PW, D), 1.0, 6.0, ((0, 2), (1, 4), (3, 4)))
    cotangent = noise(splits[1], (CROPS, GH, PW, D), 1.0, 6.0, ((0, 2), (1, 4), (3, 4)))
    weight_in = noise(splits[2], (BS, FB, NNZ, BS), (NNZ * BS) ** -0.5, 0.15625, ((0, 4), (1, 4)))
    weight_out = noise(splits[3], (BS, FB, NNZ, BS), (FB * NNZ * BS * BS // D) ** -0.5, 0.078125, ((0, 4), (1, 4)))
    mix_kernel = noise(splits[4], (9, F), 0.35, 4.0, ((1, 4),), jnp.float32)
    block_rows = draw_block_rows(jax.random.fold_in(splits[6], 71), 0)
    return dict(tokens=tokens, cotangent=cotangent, weight_in=weight_in, weight_out=weight_out, mix_kernel=mix_kernel, block_rows=block_rows)


root_two_pi = 0.7978845608
cubic_coef = 0.044715
loss_scale = 0.03125


def gelu_pair(preact):
    inner = root_two_pi * (preact + cubic_coef * preact * preact * preact)
    tanh_val = jnp.tanh(inner)
    gelu_out = 0.5 * preact * (1.0 + tanh_val)
    slopes = 0.5 * (1.0 + tanh_val) + 0.5 * preact * (1.0 - tanh_val * tanh_val) * root_two_pi * (1.0 + 3.0 * cubic_coef * preact * preact)
    return gelu_out, slopes


def reference(tokens, cotangent, weight_in, weight_out, mix_kernel, block_rows):
    crop_count, height, grid_width, depth_all = tokens.shape
    block_count = depth_all // BS
    tok_count = crop_count * height * grid_width
    groups = crop_count * N_ROWS
    in_blocks = tokens.reshape(tok_count, block_count, BS)
    cot_blocks = cotangent.reshape(tok_count, block_count, BS)
    in_cols = jnp.moveaxis(weight_in, 1, 0)
    out_cols = jnp.moveaxis(weight_out, 1, 0)
    kern_cols = jnp.transpose(mix_kernel.reshape(9, FB, BS), (1, 0, 2))

    def column(dx_carry, slices):
        in_panel, out_panel, kern_local, row_ids = slices
        in_select = jnp.take(in_blocks, row_ids, axis=1).astype(jnp.float32)
        grad_select = jnp.take(cot_blocks, row_ids, axis=1).astype(jnp.float32)
        pre_act = jnp.einsum('nkb,bke->ne', in_select, in_panel.astype(jnp.float32))
        gelu_out, slopes = gelu_pair(pre_act)
        active = gelu_out.astype(jnp.bfloat16).astype(jnp.float32).reshape(crop_count, height, grid_width, BS)
        padded = jnp.pad(active, ((0, 0), (1, 1), (1, 1), (0, 0)))
        mix_sum = jnp.zeros((crop_count, height, grid_width, BS), jnp.float32)
        for row_off in range(3):
            for col_off in range(3):
                mix_sum = mix_sum + kern_local[3 * row_off + col_off] * padded[:, row_off:row_off + height, col_off:col_off + grid_width]
        mix_out = mix_sum.astype(jnp.bfloat16).astype(jnp.float32).reshape(tok_count, BS)
        mix_grad = jnp.einsum('nkd,fkd->nf', grad_select, out_panel.astype(jnp.float32)).astype(jnp.bfloat16).astype(jnp.float32)
        grad_grid = mix_grad.reshape(crop_count, height, grid_width, BS)
        grad_pad = jnp.pad(grad_grid, ((0, 0), (1, 1), (1, 1), (0, 0)))
        act_grad = jnp.zeros((crop_count, height, grid_width, BS), jnp.float32)
        kern_terms = []
        for row_off in range(3):
            for col_off in range(3):
                act_grad = act_grad + kern_local[3 * row_off + col_off] * grad_pad[:, 2 - row_off:2 - row_off + height, 2 - col_off:2 - col_off + grid_width]
                kern_terms.append(jnp.sum(padded[:, row_off:row_off + height, col_off:col_off + grid_width] * grad_grid, axis=(0, 1, 2)))
        kern_sum = jnp.stack(kern_terms, axis=0) * loss_scale
        pre_grad = (act_grad.reshape(tok_count, BS) * slopes).astype(jnp.bfloat16).astype(jnp.float32)
        mix_groups = mix_out.reshape(groups, tok_count // groups, BS)
        cot_groups = grad_select.reshape(groups, tok_count // groups, NNZ, BS)
        out_parts = (jnp.einsum('gtf,gtkd->gfkd', mix_groups, cot_groups) * loss_scale).astype(jnp.bfloat16).astype(jnp.float32)
        in_groups = in_select.reshape(groups, tok_count // groups, NNZ, BS)
        pre_groups = pre_grad.reshape(groups, tok_count // groups, BS)
        in_parts = (jnp.einsum('gtkb,gte->gbke', in_groups, pre_groups) * loss_scale).astype(jnp.bfloat16).astype(jnp.float32)
        back_select = jnp.einsum('ne,bke->nkb', pre_grad, in_panel.astype(jnp.float32))
        dx_carry = dx_carry.at[:, row_ids].add(back_select)
        return dx_carry, (jnp.sum(in_parts, axis=0), jnp.sum(out_parts, axis=0), kern_sum)

    dx_start = jnp.zeros((tok_count, block_count, BS), jnp.float32)
    dx_total, (in_grads, out_grads, kern_grads) = lax.scan(column, dx_start, (in_cols, out_cols, kern_cols, block_rows))
    grad_tokens = dx_total.reshape(crop_count, height, grid_width, depth_all).astype(jnp.bfloat16)
    grad_w_in = jnp.moveaxis(in_grads, 0, 1)
    grad_w_out = jnp.moveaxis(out_grads, 0, 1)
    grad_kernel = jnp.transpose(kern_grads, (1, 0, 2)).reshape(9, FB * BS)
    return grad_tokens, grad_w_in, grad_w_out, grad_kernel
```

```python
import functools

import jax
import jax.numpy as jnp
from jax import lax
from jax.experimental import pallas as pl
from jax.experimental.pallas import tpu as pltpu
from jax.sharding import PartitionSpec as P

root_two_pi = 0.7978845608
cubic_coef = 0.044715
loss_scale = 0.03125

MESH_ID = pl.DeviceIdType.MESH
ANY = pl.BlockSpec(memory_space=pl.ANY)
VMEM = pl.BlockSpec(memory_space=pltpu.VMEM)
SMEM = pl.BlockSpec(memory_space=pltpu.SMEM)


def span(start, size):
    return pl.ds(pl.multiple_of(start * size, size), size)


def neighbours():
    y, r, z = lax.axis_index("crop"), lax.axis_index("rows"), lax.axis_index("hid")
    x, core = r // 2, r % 2
    same_chip = x * 2 + (1 - core)
    across = (1 - x) * 2 + core
    diagonal = (1 - x) * 2 + (1 - core)
    return y, r, z, same_chip, across, diagonal


def enter(partners):
    barrier = pltpu.get_barrier_semaphore()
    for partner in partners:
        pl.semaphore_signal(barrier, inc=1, device_id=partner, device_id_type=MESH_ID)
    pl.semaphore_wait(barrier, len(partners))


def remote(src, dst, send_sem, recv_sem, target):
    return pltpu.make_async_remote_copy(
        src_ref=src,
        dst_ref=dst,
        send_sem=send_sem,
        recv_sem=recv_sem,
        device_id=target,
        device_id_type=MESH_ID,
    )


def gather_kernel(
    depth, tok, cot, w_in, w_out, tok_all, cot_all, in_all, out_all,
    tok_send, tok_recv, w_send, w_recv, own_sem,
):
    y, r, z, same_chip, across, diagonal = neighbours()
    tokens, features = tok.shape
    rows = w_in.shape[0]
    lanes = in_all.shape[1]
    half = rows // 2
    enter(
        [{"rows": same_chip}, {"rows": across}, {"rows": diagonal}, {"crop": 1 - y}]
        + [{"hid": (z + step) % depth} for step in range(1, depth)]
    )
    streams = ((tok, tok_all), (cot, cot_all))
    panels = ((w_in, in_all), (w_out, out_all))
    started, local = [], []

    def piece(full, row, col):
        return full.at[span(row, tokens), span(col, features)]

    def send_piece(a, src, row, col, slot, target):
        copy = remote(
            src, piece(streams[a][1], row, col), tok_send.at[a, slot], tok_recv.at[a, row, col], target
        )
        copy.start()
        started.append(copy)

    def await_piece(a, row, col):
        part = piece(streams[a][1], row, col)
        remote(
            part, part, tok_send.at[a, 0], tok_recv.at[a, row, col], {"rows": same_chip}
        ).wait_recv()
        return part

    def half_rows(full, row, h):
        return full.at[pl.ds(pl.multiple_of(row * rows + h * half, half), half), :]

    for a in range(2):
        src = streams[a][0]
        for step in range(1, depth):
            send_piece(a, src, r, z, step - 1, {"hid": (z + step) % depth})
        send_piece(a, src, r, z, depth - 1, {"rows": across})
    for a in range(2):
        src, full = panels[a]
        for slot, dest in ((1, across), (2, diagonal)):
            copy = remote(
                src.at[span(y, half), span(dest, lanes)],
                half_rows(full, r, y),
                w_send.at[a, slot],
                w_recv.at[a, r, y],
                {"rows": dest},
            )
            copy.start()
            started.append(copy)
        copy = remote(
            src.at[:, span(same_chip, lanes)],
            full.at[span(r, rows), :],
            w_send.at[a, 0],
            w_recv.at[a, r, 0],
            {"rows": same_chip},
        )
        copy.start()
        started.append(copy)
        send_piece(a, streams[a][0], r, z, depth, {"rows": same_chip})
        local.append(pltpu.make_async_copy(streams[a][0], piece(streams[a][1], r, z), own_sem.at[a, 0]))
        local.append(
            pltpu.make_async_copy(
                src.at[:, span(r, lanes)], full.at[span(r, rows), :], own_sem.at[a, 1]
            )
        )
    for copy in local:
        copy.start()
    for step in range(1, depth):
        col = (z + step) % depth
        for a in range(2):
            part = await_piece(a, r, col)
            send_piece(a, part, r, col, depth + 2 * step - 1, {"rows": across})
            send_piece(a, part, r, col, depth + 2 * step, {"rows": same_chip})
    for a in range(2):
        full = panels[a][1]
        for slot, row in ((3, across), (4, diagonal)):
            part = half_rows(full, row, y)
            copy = remote(
                part, part, w_send.at[a, slot], w_recv.at[a, row, y], {"rows": row}
            )
            copy.wait_recv()
            copy = remote(
                part, part, w_send.at[a, slot], w_recv.at[a, row, y], {"crop": 1 - y}
            )
            copy.start()
            started.append(copy)
    for step in range(depth):
        col = (z + step) % depth
        for a in range(2):
            part = await_piece(a, across, col)
            send_piece(a, part, across, col, 3 * depth - 1 + step, {"rows": same_chip})
    for a in range(2):
        full = panels[a][1]
        part = full.at[span(same_chip, rows), :]
        remote(
            part, part, w_send.at[a, 0], w_recv.at[a, same_chip, 0], {"rows": same_chip}
        ).wait_recv()
        for row in (across, diagonal):
            part = half_rows(full, row, 1 - y)
            remote(
                part, part, w_send.at[a, 0], w_recv.at[a, row, 1 - y], {"crop": 1 - y}
            ).wait_recv()
        for row in (same_chip, diagonal):
            for step in range(depth):
                await_piece(a, row, (z + step) % depth)
    for copy in local:
        copy.wait()
    for copy in started:
        copy.wait_send()


def nt(a, b):
    return lax.dot_general(a, b, (((1,), (1,)), ((), ())), preferred_element_type=jnp.float32)


def tn(a, b):
    return lax.dot_general(a, b, (((0,), (0,)), ((), ())), preferred_element_type=jnp.float32)


def local_kernel(
    width, block, cols, nnz, ids, tok, cot, w_in, w_out, taps,
    dx_out, gw_in, gw_out, kern, dx, pre_s, act_s, slope_s, mg_s,
):
    count = tok.shape[0]
    dx[...] = jnp.zeros_like(dx)
    place = lax.broadcasted_iota(jnp.int32, (count, block), 0) % width
    kern[...] = jnp.zeros_like(kern)

    def spread(value):
        before = jnp.where(place == 0, 0.0, pltpu.roll(value, 1, 0))
        after = jnp.where(place == width - 1, 0.0, pltpu.roll(value, count - 1, 0))
        return (before, value, after)

    def stack_rows(up, mid, down):
        edge = jnp.zeros((width, block), jnp.float32)
        return (
            mid
            + jnp.concatenate([edge, up[:-width]], axis=0)
            + jnp.concatenate([down[width:], edge], axis=0)
        )

    def column(c, carry):
        hidden = span(c, block)

        def feats(k):
            return span(ids[c * nnz + k], block)

        def panel(k):
            return span(c * nnz + k, block)

        pre = jnp.dot(tok[:, feats(0)], w_in[:, panel(0)], preferred_element_type=jnp.float32)
        for k in range(1, nnz):
            pre += jnp.dot(tok[:, feats(k)], w_in[:, panel(k)], preferred_element_type=jnp.float32)
        pre_s[...] = pre
        mg = nt(cot[:, feats(0)], w_out[:, panel(0)])
        for k in range(1, nnz):
            mg += nt(cot[:, feats(k)], w_out[:, panel(k)])
        mg_s[...] = mg.astype(jnp.bfloat16).astype(jnp.float32)
        p = pre_s[...]
        t = jnp.tanh(root_two_pi * (p + cubic_coef * p * p * p))
        act_s[...] = (0.5 * p * (1.0 + t)).astype(jnp.bfloat16).astype(jnp.float32)
        slope_s[...] = 0.5 * (1.0 + t) + 0.5 * p * (1.0 - t * t) * root_two_pi * (
            1.0 + 3.0 * cubic_coef * p * p
        )

        def tap(a, b):
            row = 3 * (a + 1) + (b + 1)
            return taps[row : row + 1, hidden]

        acts = spread(act_s[...])
        mixed = stack_rows(
            *[sum(tap(a, b) * acts[b + 1] for b in (-1, 0, 1)) for a in (-1, 0, 1)]
        ).astype(jnp.bfloat16)
        grads = mg_s[...]
        for b in (-1, 0, 1):
            seen = acts[b + 1]
            sums = (
                jnp.sum(seen[:-width] * grads[width:], axis=0, keepdims=True),
                jnp.sum(seen * grads, axis=0, keepdims=True),
                jnp.sum(seen[width:] * grads[:-width], axis=0, keepdims=True),
            )
            for a in (-1, 0, 1):
                row = 3 * (a + 1) + (b + 1)
                kern[row : row + 1, hidden] = sums[a + 1] * loss_scale
        for k in range(nnz):
            gw_out[:, panel(k)] = (tn(mixed, cot[:, feats(k)]) * loss_scale).astype(jnp.bfloat16)
        backs = spread(mg_s[...])
        gathered = stack_rows(
            *[sum(tap(a, b) * backs[1 - b] for b in (-1, 0, 1)) for a in (1, 0, -1)]
        )
        pre_grad = (gathered * slope_s[...]).astype(jnp.bfloat16)
        for k in range(nnz):
            gw_in[:, panel(k)] = (tn(tok[:, feats(k)], pre_grad) * loss_scale).astype(jnp.bfloat16)
            dx[:, feats(k)] += nt(pre_grad, w_in[:, panel(k)])
        return carry

    lax.fori_loop(0, cols, column, 0)
    dx_out[...] = dx[...].astype(jnp.bfloat16)


def scatter_kernel(
    depth, dx, gw_in, gw_out, kern, dx_mine, in_mine, out_mine, kern_all,
    dx_near, dx_half, dx_far, dx_sum, dx_last, gw_part, gw_sum, kern_part,
    dx_send, dx_recv, gw_send, gw_recv, kern_send, kern_recv,
):
    y, r, z, same_chip, across, diagonal = neighbours()
    group = [same_chip, across, diagonal]
    enter(
        [{"rows": row} for row in group]
        + [{"crop": 1 - y, "rows": row} for row in group]
        + [{"crop": 1 - y}]
        + [{"hid": (z + step) % depth} for step in range(1, depth)]
    )
    started = []

    def go(*args):
        copy = remote(*args)
        copy.start()
        started.append(copy)

    tokens, features = dx_mine.shape
    rows = in_mine.shape[0]
    lanes = gw_in.shape[1]
    weights = ((gw_in, in_mine), (gw_out, out_mine))
    for slot, row in enumerate((diagonal, same_chip)):
        go(dx.at[span(row, tokens), :], dx_near.at[slot], dx_send.at[slot], dx_recv.at[slot], {"rows": same_chip})
    order = (across, diagonal, same_chip, r)
    for slot, row in enumerate(order):
        for a in range(2):
            go(
                weights[a][0].at[span((1 - y) * 4 + row, rows), :],
                gw_part.at[a, slot],
                gw_send.at[a, slot],
                gw_recv.at[a, slot],
                {"crop": 1 - y},
            )
    for slot, row in enumerate(group):
        go(kern, kern_part.at[y, r], kern_send.at[slot], kern_recv.at[y, r], {"rows": row})
        go(
            kern,
            kern_part.at[y, r],
            kern_send.at[slot + 3],
            kern_recv.at[y, r],
            {"crop": 1 - y, "rows": row},
        )
    go(kern, kern_part.at[y, r], kern_send.at[6], kern_recv.at[y, r], {"crop": 1 - y})

    def arrived(ref, send_sem, recv_sem, target):
        remote(ref, ref, send_sem, recv_sem, target).wait_recv()

    arrived(dx_near.at[0], dx_send.at[0], dx_recv.at[0], {"rows": same_chip})
    dx_half[...] = (
        dx[span(across, tokens), :].astype(jnp.float32) + dx_near[0].astype(jnp.float32)
    ).astype(jnp.bfloat16)
    go(dx_half, dx_far, dx_send.at[2], dx_recv.at[2], {"rows": across})
    arrived(dx_near.at[1], dx_send.at[1], dx_recv.at[1], {"rows": same_chip})
    arrived(dx_far, dx_send.at[2], dx_recv.at[2], {"rows": across})
    for col in range(depth):
        part = slice(col * features, (col + 1) * features)
        dx_sum[col] = (
            dx[span(r, tokens), part].astype(jnp.float32)
            + dx_near[1, :, part].astype(jnp.float32)
            + dx_far[:, part].astype(jnp.float32)
        ).astype(jnp.bfloat16)
    for step in range(1, depth):
        go(
            dx_sum.at[(z + step) % depth],
            dx_last.at[step - 1],
            dx_send.at[2 + step],
            dx_recv.at[2 + step],
            {"hid": (z + step) % depth},
        )
    for slot, row in enumerate(order):
        for a in range(2):
            arrived(gw_part.at[a, slot], gw_send.at[a, slot], gw_recv.at[a, slot], {"crop": 1 - y})
            total = (
                weights[a][0][span(y * 4 + row, rows), :].astype(jnp.float32)
                + gw_part[a, slot].astype(jnp.float32)
            ).astype(jnp.bfloat16)
            if slot == 3:
                weights[a][1][:, span(r, lanes)] = total
            else:
                gw_sum[a, slot] = total
                go(
                    gw_sum.at[a, slot],
                    weights[a][1].at[:, span(r, lanes)],
                    gw_send.at[a, 4 + slot],
                    gw_recv.at[a, 4 + slot],
                    {"rows": row},
                )
    total = dx_sum[z].astype(jnp.float32)
    for step in range(1, depth):
        arrived(dx_last.at[step - 1], dx_send.at[2 + step], dx_recv.at[2 + step], {"hid": (z + step) % depth})
        total += dx_last[step - 1].astype(jnp.float32)
    dx_mine[...] = total.astype(jnp.bfloat16)
    kern_part[y, r] = kern[...]
    for row in group:
        for crop in (y, 1 - y):
            arrived(kern_part.at[crop, row], kern_send.at[0], kern_recv.at[crop, row], {"rows": same_chip})
    arrived(kern_part.at[1 - y, r], kern_send.at[0], kern_recv.at[1 - y, r], {"rows": same_chip})
    wide = kern.shape[1]
    for row in range(4):
        kern_all[:, row * wide : (row + 1) * wide] = kern_part[0, row].astype(
            jnp.float32
        ) + kern_part[1, row].astype(jnp.float32)
    for slot, row in enumerate(order[:3]):
        for a in range(2):
            arrived(
                weights[a][1].at[:, span(row, lanes)],
                gw_send.at[a, 4 + slot],
                gw_recv.at[a, 4 + slot],
                {"rows": row},
            )
    for copy in started:
        copy.wait_send()


def split_hidden(tokens, cotangent, weight_in, weight_out, mix_kernel, block_rows):
    n_rows, depth = lax.axis_size("rows"), lax.axis_size("hid")
    _, height, width, features = tokens.shape
    rows, all_cols, nnz, block = weight_in.shape
    count = height * width
    whole = count * n_rows
    model = features * depth
    cols = all_cols // n_rows
    lanes = cols * nnz * block
    hidden = cols * block
    bf16, f32 = jnp.bfloat16, jnp.float32
    dma, sds = pltpu.SemaphoreType.DMA, jax.ShapeDtypeStruct
    params = functools.partial(pltpu.CompilerParams, vmem_limit_bytes=60 * 1024 * 1024)
    tok_all, cot_all, in_all, out_all = pl.pallas_call(
        functools.partial(gather_kernel, depth),
        name="gather_parts",
        out_shape=[sds((whole, model), bf16)] * 2 + [sds((rows * n_rows, lanes), bf16)] * 2,
        in_specs=[ANY] * 4,
        out_specs=[ANY] * 4,
        scratch_shapes=[
            dma((2, 4 * depth)),
            dma((2, n_rows, depth)),
            dma((2, 5)),
            dma((2, n_rows, 2)),
            dma((2, 2)),
        ],
        compiler_params=pltpu.CompilerParams(collective_id=1, has_side_effects=True),
    )(
        tokens.reshape(count, features),
        cotangent.reshape(count, features),
        weight_in.reshape(rows, all_cols * nnz * block),
        weight_out.reshape(rows, all_cols * nnz * block),
    )
    me = lax.axis_index("rows")
    taps = lax.dynamic_slice_in_dim(mix_kernel, me * hidden, hidden, axis=1)
    ids = lax.dynamic_slice_in_dim(block_rows, me * cols, cols, axis=0).reshape(-1)
    dx, gw_in, gw_out, kern = pl.pallas_call(
        functools.partial(local_kernel, width, block, cols, nnz),
        name="local_math",
        out_shape=[
            sds((whole, model), bf16),
            sds((block, lanes), bf16),
            sds((block, lanes), bf16),
            sds((16, hidden), f32),
        ],
        in_specs=[SMEM] + [VMEM] * 5,
        out_specs=[VMEM] * 4,
        scratch_shapes=[pltpu.VMEM((whole, model), f32)] + [pltpu.VMEM((whole, block), f32)] * 4,
        compiler_params=params(),
    )(ids, tok_all, cot_all, in_all, out_all, taps)
    out_rows = block // (n_rows * lax.axis_size("crop"))
    dx_mine, in_mine, out_mine, kern_all = pl.pallas_call(
        functools.partial(scatter_kernel, depth),
        name="scatter_sums",
        out_shape=[
            sds((count, features), bf16),
            sds((out_rows, all_cols * nnz * block), bf16),
            sds((out_rows, all_cols * nnz * block), bf16),
            sds((16, hidden * n_rows), f32),
        ],
        in_specs=[VMEM] * 4,
        out_specs=[VMEM] * 4,
        scratch_shapes=[
            pltpu.VMEM((2, count, model), bf16),
            pltpu.VMEM((count, model), bf16),
            pltpu.VMEM((count, model), bf16),
            pltpu.VMEM((depth, count, features), bf16),
            pltpu.VMEM((depth - 1, count, features), bf16),
            pltpu.VMEM((2, 4, out_rows, lanes), bf16),
            pltpu.VMEM((2, 3, out_rows, lanes), bf16),
            pltpu.VMEM((2, n_rows, 16, hidden), bf16),
            dma((2 + depth,)),
            dma((2 + depth,)),
            dma((2, 7)),
            dma((2, 7)),
            dma((7,)),
            dma((2, n_rows)),
        ],
        compiler_params=params(collective_id=2, has_side_effects=True),
    )(dx, gw_in, gw_out, kern.astype(bf16))
    shape = (out_rows, all_cols, nnz, block)
    return (
        dx_mine.reshape(tokens.shape),
        in_mine.astype(f32).reshape(shape),
        out_mine.astype(f32).reshape(shape),
        kern_all[: mix_kernel.shape[0]],
    )


def padded(shard, sides, width):
    for axis, dim in sides:
        devices, length = (lax.axis_size(axis), shard.shape[dim])
        up = [(i, (i + 1) % devices) for i in range(devices - 1)]
        down = [(j, i) for i, j in up]
        last = lax.slice_in_dim(shard, length - width, length, axis=dim)
        initial = lax.slice_in_dim(shard, 0, width, axis=dim)
        before = lax.ppermute(last, axis, up)
        after = lax.ppermute(initial, axis, down)
        shard = jnp.concatenate([before, shard, after], axis=dim)
    return shard


def gelu_pair(preact):
    inner = root_two_pi * (preact + cubic_coef * preact * preact * preact)
    tanh_val = jnp.tanh(inner)
    gelu_out = 0.5 * preact * (1.0 + tanh_val)
    slopes = 0.5 * (1.0 + tanh_val) + 0.5 * preact * (1.0 - tanh_val * tanh_val) * root_two_pi * (
        1.0 + 3.0 * cubic_coef * preact * preact
    )
    return (gelu_out, slopes)


def on_device(tokens, cotangent, weight_in, weight_out, mix_kernel, block_rows):
    in_panel, out_panel = (
        lax.all_gather(weight_in, "rows", axis=0, tiled=True),
        lax.all_gather(weight_out, "rows", axis=0, tiled=True),
    )
    tok_full, cot_full = (
        lax.all_gather(tokens, "hid", axis=3, tiled=True),
        lax.all_gather(cotangent, "hid", axis=3, tiled=True),
    )
    crop_count, height, grid_width, depth_all = tok_full.shape
    tok_count = crop_count * height * grid_width
    block_size = in_panel.shape[0]
    col_count = in_panel.shape[1]
    nnz_count = in_panel.shape[2]
    block_count = depth_all // block_size
    hidden_local = col_count * block_size
    flat_rows = block_rows.reshape(-1)
    in_select = jnp.take(
        tok_full.reshape(tok_count, block_count, block_size), flat_rows, axis=1
    ).reshape(tok_count, col_count, nnz_count, block_size)
    grad_select = jnp.take(
        cot_full.reshape(tok_count, block_count, block_size), flat_rows, axis=1
    ).reshape(tok_count, col_count, nnz_count, block_size)
    pre_act = jnp.einsum("tckb,bcke->tce", in_select, in_panel, preferred_element_type=jnp.float32)
    gelu_out, slopes = gelu_pair(pre_act)
    active = gelu_out.astype(jnp.bfloat16).reshape(crop_count, height, grid_width, hidden_local)
    act_rim = padded(active, (("rows", 1),), 1)
    mix_grad = (
        jnp.einsum("tckd,fckd->tcf", grad_select, out_panel, preferred_element_type=jnp.float32)
        .astype(jnp.bfloat16)
        .reshape(crop_count, height, grid_width, hidden_local)
    )
    grad_rim = padded(mix_grad, (("rows", 1),), 1)
    act_pad = jnp.pad(act_rim.astype(jnp.float32), ((0, 0), (0, 0), (1, 1), (0, 0)))
    grad_pad = jnp.pad(grad_rim.astype(jnp.float32), ((0, 0), (0, 0), (1, 1), (0, 0)))
    grad_grid = mix_grad.astype(jnp.float32)
    mix_sum = jnp.zeros((crop_count, height, grid_width, hidden_local), jnp.float32)
    act_grad = jnp.zeros((crop_count, height, grid_width, hidden_local), jnp.float32)
    kern_terms = []
    for row_off in range(3):
        for col_off in range(3):
            tap = mix_kernel[3 * row_off + col_off]
            shifted = act_pad[:, row_off : row_off + height, col_off : col_off + grid_width]
            mix_sum = mix_sum + tap * shifted
            act_grad = (
                act_grad
                + tap
                * grad_pad[
                    :, 2 - row_off : 2 - row_off + height, 2 - col_off : 2 - col_off + grid_width
                ]
            )
            kern_terms.append(jnp.sum(shifted * grad_grid, axis=(0, 1, 2)))
    kern_local = jnp.stack(kern_terms, axis=0) * loss_scale
    mix_out = mix_sum.astype(jnp.bfloat16).reshape(tok_count, col_count, block_size)
    pre_grad = (act_grad.reshape(tok_count, col_count, block_size) * slopes).astype(jnp.bfloat16)
    kern_total = lax.psum(kern_local.astype(jnp.bfloat16), ("crop", "rows")).astype(jnp.float32)
    back_select = jnp.einsum(
        "tce,bcke->tckb", pre_grad, in_panel, preferred_element_type=jnp.float32
    )
    one_hot = (
        block_rows[:, :, None] == jnp.arange(block_count, dtype=jnp.int32)[None, None, :]
    ).astype(jnp.float32)
    token_terms = jnp.einsum(
        "tckb,ckr->trb", back_select, one_hot, precision=lax.Precision.HIGHEST
    ).reshape(crop_count, height, grid_width, depth_all)
    grad_tokens = lax.psum_scatter(
        token_terms.astype(jnp.bfloat16), "hid", scatter_dimension=3, tiled=True
    )
    first_term = jnp.einsum(
        "tckb,tce->bcke", in_select, pre_grad, preferred_element_type=jnp.float32
    )
    second_term = jnp.einsum(
        "tcf,tckd->fckd", mix_out, grad_select, preferred_element_type=jnp.float32
    )
    share_sums = lax.psum_scatter(
        (jnp.stack([first_term, second_term], axis=1) * loss_scale).astype(jnp.bfloat16),
        ("crop", "rows"),
        scatter_dimension=0,
        tiled=True,
    ).astype(jnp.float32)
    return (grad_tokens, share_sums[:, 0], share_sums[:, 1], kern_total)


def solution(mesh):
    placed = (
        P("crop", "rows", None, "hid"),
        P("crop", "rows", None, "hid"),
        P("rows", "hid", None, None),
        P("rows", "hid", None, None),
        P(None, "hid"),
        P("hid", None),
    )
    n_crop, n_rows = mesh.shape["crop"], mesh.shape["rows"]
    n_hid = mesh.shape["hid"]

    def step(tokens, cotangent, weight_in, weight_out, mix_kernel, block_rows):
        fits = (
            n_crop == 2
            and n_rows == 4
            and tokens.shape[0] == 1
            and weight_in.shape[1] % n_rows == 0
            and tokens.shape[1] * tokens.shape[2] * n_rows * tokens.shape[3] * n_hid <= 2**22
        )
        chosen = split_hidden if fits else on_device
        return chosen(tokens, cotangent, weight_in, weight_out, mix_kernel, block_rows)

    return jax.shard_map(
        step,
        mesh=mesh,
        in_specs=placed,
        out_specs=(
            P("crop", "rows", None, "hid"),
            P(("crop", "rows"), "hid", None, None),
            P(("crop", "rows"), "hid", None, None),
            P(None, "hid"),
        ),
        check_vma=False,
    )
```

```python
import functools

import jax
import jax.numpy as jnp
from jax import lax
from jax.experimental import pallas as pl
from jax.experimental.pallas import tpu as pltpu
from jax.sharding import PartitionSpec as P

root_two_pi = 0.7978845608
cubic_coef = 0.044715
loss_scale = 0.03125

MESH_ID = pl.DeviceIdType.MESH
ANY = pl.BlockSpec(memory_space=pl.ANY)
VMEM = pl.BlockSpec(memory_space=pltpu.VMEM)
SMEM = pl.BlockSpec(memory_space=pltpu.SMEM)


def span(start, size):
    return pl.ds(pl.multiple_of(start * size, size), size)


def neighbours():
    y, r, z = lax.axis_index("crop"), lax.axis_index("rows"), lax.axis_index("hid")
    x, core = r // 2, r % 2
    same_chip = x * 2 + (1 - core)
    across = (1 - x) * 2 + core
    diagonal = (1 - x) * 2 + (1 - core)
    return y, r, z, same_chip, across, diagonal


def enter(partners):
    barrier = pltpu.get_barrier_semaphore()
    for partner in partners:
        pl.semaphore_signal(barrier, inc=1, device_id=partner, device_id_type=MESH_ID)
    pl.semaphore_wait(barrier, len(partners))


def remote(src, dst, send_sem, recv_sem, target):
    return pltpu.make_async_remote_copy(
        src_ref=src,
        dst_ref=dst,
        send_sem=send_sem,
        recv_sem=recv_sem,
        device_id=target,
        device_id_type=MESH_ID,
    )


def gather_kernel(
    depth, tok, cot, w_in, w_out, tok_all, cot_all, in_all, out_all,
    raw, flat, stage, tok_send, tok_recv, w_send, w_recv, own_sem, raw_sem,
):
    y, r, z, same_chip, across, diagonal = neighbours()
    tokens, features = tok.shape
    rows = w_in.shape[0]
    lanes = in_all.shape[1]
    half = rows // 2
    block = w_in.shape[2]
    all_cols = stage.shape[1] // rows
    nnz = w_in.shape[1] // all_cols
    loads = [
        pltpu.make_async_copy(src, raw.at[a], raw_sem.at[a]) for a, src in enumerate((w_in, w_out))
    ]
    for load in loads:
        load.start()
    enter(
        [{"rows": same_chip}, {"rows": across}, {"rows": diagonal}, {"crop": 1 - y}]
        + [{"hid": (z + step) % depth} for step in range(1, depth)]
    )
    streams = ((tok, tok_all), (cot, cot_all))
    panels = ((flat.at[0], in_all), (flat.at[1], out_all))
    started, local = [], []

    def piece(full, row, col):
        return full.at[span(row, tokens), span(col, features)]

    def send_piece(a, src, row, col, slot, target):
        copy = remote(
            src, piece(streams[a][1], row, col), tok_send.at[a, slot], tok_recv.at[a, row, col], target
        )
        copy.start()
        started.append(copy)

    def await_piece(a, row, col):
        part = piece(streams[a][1], row, col)
        remote(
            part, part, tok_send.at[a, 0], tok_recv.at[a, row, col], {"rows": same_chip}
        ).wait_recv()
        return part

    def half_rows(full, row, h):
        return full.at[pl.ds(pl.multiple_of(row * rows + h * half, half), half), :]

    for a in range(2):
        src = streams[a][0]
        for step in range(1, depth):
            send_piece(a, src, r, z, step - 1, {"hid": (z + step) % depth})
        send_piece(a, src, r, z, depth - 1, {"rows": across})
        send_piece(a, src, r, z, depth, {"rows": same_chip})
        local.append(pltpu.make_async_copy(src, piece(streams[a][1], r, z), own_sem.at[a, 0]))
        local[-1].start()

    def flatten(a):
        def turn(k, carry):
            for h in range(block // 128):
                part = raw[a, :, span(k, all_cols), h * 128 : (h + 1) * 128]
                stage[h] = part.astype(jnp.float32).reshape(rows * all_cols, 128)
            for c in range(all_cols):
                for h in range(block // 128):
                    flat[a, :, pl.ds(pl.multiple_of((c * nnz + k) * block + h * 128, 128), 128)] = stage[
                        h, pl.ds(c, rows, stride=all_cols), :
                    ].astype(jnp.bfloat16)
            return carry

        lax.fori_loop(0, nnz, turn, 0)

    for a in range(2):
        src, full = panels[a]
        loads[a].wait()
        flatten(a)
        for slot, dest in ((1, across), (2, diagonal)):
            copy = remote(
                src.at[span(y, half), span(dest, lanes)],
                half_rows(full, r, y),
                w_send.at[a, slot],
                w_recv.at[a, r, y],
                {"rows": dest},
            )
            copy.start()
            started.append(copy)
        copy = remote(
            src.at[:, span(same_chip, lanes)],
            full.at[span(r, rows), :],
            w_send.at[a, 0],
            w_recv.at[a, r, 0],
            {"rows": same_chip},
        )
        copy.start()
        started.append(copy)
        local.append(
            pltpu.make_async_copy(
                src.at[:, span(r, lanes)], full.at[span(r, rows), :], own_sem.at[a, 1]
            )
        )
        local[-1].start()
    for step in range(1, depth):
        col = (z + step) % depth
        for a in range(2):
            part = await_piece(a, r, col)
            send_piece(a, part, r, col, depth + 2 * step - 1, {"rows": across})
            send_piece(a, part, r, col, depth + 2 * step, {"rows": same_chip})
    for a in range(2):
        full = panels[a][1]
        for slot, row in ((3, across), (4, diagonal)):
            part = half_rows(full, row, y)
            copy = remote(
                part, part, w_send.at[a, slot], w_recv.at[a, row, y], {"rows": row}
            )
            copy.wait_recv()
            copy = remote(
                part, part, w_send.at[a, slot], w_recv.at[a, row, y], {"crop": 1 - y}
            )
            copy.start()
            started.append(copy)
    for step in range(depth):
        col = (z + step) % depth
        for a in range(2):
            part = await_piece(a, across, col)
            send_piece(a, part, across, col, 3 * depth - 1 + step, {"rows": same_chip})
    for a in range(2):
        full = panels[a][1]
        part = full.at[span(same_chip, rows), :]
        remote(
            part, part, w_send.at[a, 0], w_recv.at[a, same_chip, 0], {"rows": same_chip}
        ).wait_recv()
        for row in (across, diagonal):
            part = half_rows(full, row, 1 - y)
            remote(
                part, part, w_send.at[a, 0], w_recv.at[a, row, 1 - y], {"crop": 1 - y}
            ).wait_recv()
        for row in (same_chip, diagonal):
            for step in range(depth):
                await_piece(a, row, (z + step) % depth)
    for copy in local:
        copy.wait()
    for copy in started:
        copy.wait_send()


def nt(a, b):
    return lax.dot_general(a, b, (((1,), (1,)), ((), ())), preferred_element_type=jnp.float32)


def tn(a, b):
    return lax.dot_general(a, b, (((0,), (0,)), ((), ())), preferred_element_type=jnp.float32)


def local_kernel(
    width, block, cols, nnz, ids, tok, cot, w_in, w_out, taps,
    dx_out, gw_in, gw_out, kern_out, kern, dx, pre_s, act_s, slope_s, mg_s,
):
    count = tok.shape[0]
    me = lax.axis_index("rows")
    dx[...] = jnp.zeros_like(dx)
    place = lax.broadcasted_iota(jnp.int32, (count, block), 0) % width
    kern[...] = jnp.zeros_like(kern)

    def spread(value):
        before = jnp.where(place == 0, 0.0, pltpu.roll(value, 1, 0))
        after = jnp.where(place == width - 1, 0.0, pltpu.roll(value, count - 1, 0))
        return (before, value, after)

    def stack_rows(up, mid, down):
        edge = jnp.zeros((width, block), jnp.float32)
        return (
            mid
            + jnp.concatenate([edge, up[:-width]], axis=0)
            + jnp.concatenate([down[width:], edge], axis=0)
        )

    def column(c, carry):
        hidden = span(c, block)

        def feats(k):
            return span(ids[me * cols + c, k], block)

        def panel(k):
            return span(c * nnz + k, block)

        pre = jnp.dot(tok[:, feats(0)], w_in[:, panel(0)], preferred_element_type=jnp.float32)
        for k in range(1, nnz):
            pre += jnp.dot(tok[:, feats(k)], w_in[:, panel(k)], preferred_element_type=jnp.float32)
        pre_s[...] = pre
        mg = nt(cot[:, feats(0)], w_out[:, panel(0)])
        for k in range(1, nnz):
            mg += nt(cot[:, feats(k)], w_out[:, panel(k)])
        mg_s[...] = mg.astype(jnp.bfloat16).astype(jnp.float32)
        p = pre_s[...]
        t = jnp.tanh(root_two_pi * (p + cubic_coef * p * p * p))
        act_s[...] = (0.5 * p * (1.0 + t)).astype(jnp.bfloat16).astype(jnp.float32)
        slope_s[...] = 0.5 * (1.0 + t) + 0.5 * p * (1.0 - t * t) * root_two_pi * (
            1.0 + 3.0 * cubic_coef * p * p
        )

        def tap(a, b):
            row = 3 * (a + 1) + (b + 1)
            return taps[row : row + 1, span(me * cols + c, block)]

        acts = spread(act_s[...])
        mixed = stack_rows(
            *[sum(tap(a, b) * acts[b + 1] for b in (-1, 0, 1)) for a in (-1, 0, 1)]
        ).astype(jnp.bfloat16)
        grads = mg_s[...]
        for b in (-1, 0, 1):
            seen = acts[b + 1]
            sums = (
                jnp.sum(seen[:-width] * grads[width:], axis=0, keepdims=True),
                jnp.sum(seen * grads, axis=0, keepdims=True),
                jnp.sum(seen[width:] * grads[:-width], axis=0, keepdims=True),
            )
            for a in (-1, 0, 1):
                row = 3 * (a + 1) + (b + 1)
                kern[row : row + 1, hidden] = sums[a + 1] * loss_scale
        for k in range(nnz):
            gw_out[:, panel(k)] = (tn(mixed, cot[:, feats(k)]) * loss_scale).astype(jnp.bfloat16)
        backs = spread(mg_s[...])
        gathered = stack_rows(
            *[sum(tap(a, b) * backs[1 - b] for b in (-1, 0, 1)) for a in (1, 0, -1)]
        )
        pre_grad = (gathered * slope_s[...]).astype(jnp.bfloat16)
        for k in range(nnz):
            gw_in[:, panel(k)] = (tn(tok[:, feats(k)], pre_grad) * loss_scale).astype(jnp.bfloat16)
            dx[:, feats(k)] += nt(pre_grad, w_in[:, panel(k)])
        return carry

    lax.fori_loop(0, cols, column, 0)
    dx_out[...] = dx[...].astype(jnp.bfloat16)
    kern_out[...] = kern[...].astype(jnp.bfloat16)


def scatter_kernel(
    depth, dx, gw_in, gw_out, kern, dx_mine, in_mine, out_mine, kern_all,
    dx_near, dx_half, dx_far, dx_sum, dx_last, gw_part, gw_sum, kern_part,
    dx_send, dx_recv, gw_send, gw_recv, kern_send, kern_recv,
):
    y, r, z, same_chip, across, diagonal = neighbours()
    group = [same_chip, across, diagonal]
    enter(
        [{"rows": row} for row in group]
        + [{"crop": 1 - y, "rows": row} for row in group]
        + [{"crop": 1 - y}]
        + [{"hid": (z + step) % depth} for step in range(1, depth)]
    )
    started = []

    def go(*args):
        copy = remote(*args)
        copy.start()
        started.append(copy)

    tokens, features = dx_mine.shape
    rows = in_mine.shape[0]
    lanes = gw_in.shape[1]
    weights = ((gw_in, in_mine), (gw_out, out_mine))
    for slot, row in enumerate((diagonal, same_chip)):
        go(dx.at[span(row, tokens), :], dx_near.at[slot], dx_send.at[slot], dx_recv.at[slot], {"rows": same_chip})
    order = (across, diagonal, same_chip, r)
    for slot, row in enumerate(order):
        for a in range(2):
            go(
                weights[a][0].at[span((1 - y) * 4 + row, rows), :],
                gw_part.at[a, slot],
                gw_send.at[a, slot],
                gw_recv.at[a, slot],
                {"crop": 1 - y},
            )
    for slot, row in enumerate(group):
        go(kern, kern_part.at[y, r], kern_send.at[slot], kern_recv.at[y, r], {"rows": row})
        go(
            kern,
            kern_part.at[y, r],
            kern_send.at[slot + 3],
            kern_recv.at[y, r],
            {"crop": 1 - y, "rows": row},
        )
    go(kern, kern_part.at[y, r], kern_send.at[6], kern_recv.at[y, r], {"crop": 1 - y})

    def arrived(ref, send_sem, recv_sem, target):
        remote(ref, ref, send_sem, recv_sem, target).wait_recv()

    arrived(dx_near.at[0], dx_send.at[0], dx_recv.at[0], {"rows": same_chip})
    dx_half[...] = (
        dx[span(across, tokens), :].astype(jnp.float32) + dx_near[0].astype(jnp.float32)
    ).astype(jnp.bfloat16)
    go(dx_half, dx_far, dx_send.at[2], dx_recv.at[2], {"rows": across})
    arrived(dx_near.at[1], dx_send.at[1], dx_recv.at[1], {"rows": same_chip})
    arrived(dx_far, dx_send.at[2], dx_recv.at[2], {"rows": across})
    for col in range(depth):
        part = slice(col * features, (col + 1) * features)
        dx_sum[col] = (
            dx[span(r, tokens), part].astype(jnp.float32)
            + dx_near[1, :, part].astype(jnp.float32)
            + dx_far[:, part].astype(jnp.float32)
        ).astype(jnp.bfloat16)
    for step in range(1, depth):
        go(
            dx_sum.at[(z + step) % depth],
            dx_last.at[step - 1],
            dx_send.at[2 + step],
            dx_recv.at[2 + step],
            {"hid": (z + step) % depth},
        )
    for slot, row in enumerate(order):
        for a in range(2):
            arrived(gw_part.at[a, slot], gw_send.at[a, slot], gw_recv.at[a, slot], {"crop": 1 - y})
            total = (
                weights[a][0][span(y * 4 + row, rows), :].astype(jnp.float32)
                + gw_part[a, slot].astype(jnp.float32)
            ).astype(jnp.bfloat16)
            if slot == 3:
                weights[a][1][:, span(r, lanes)] = total
            else:
                gw_sum[a, slot] = total
                go(
                    gw_sum.at[a, slot],
                    weights[a][1].at[:, span(r, lanes)],
                    gw_send.at[a, 4 + slot],
                    gw_recv.at[a, 4 + slot],
                    {"rows": row},
                )
    total = dx_sum[z].astype(jnp.float32)
    for step in range(1, depth):
        arrived(dx_last.at[step - 1], dx_send.at[2 + step], dx_recv.at[2 + step], {"hid": (z + step) % depth})
        total += dx_last[step - 1].astype(jnp.float32)
    dx_mine[...] = total.astype(jnp.bfloat16)
    kern_part[y, r] = kern[...]
    for row in group:
        for crop in (y, 1 - y):
            arrived(kern_part.at[crop, row], kern_send.at[0], kern_recv.at[crop, row], {"rows": same_chip})
    arrived(kern_part.at[1 - y, r], kern_send.at[0], kern_recv.at[1 - y, r], {"rows": same_chip})
    wide = kern.shape[1]
    for row in range(4):
        kern_all[:, row * wide : (row + 1) * wide] = kern_part[0, row].astype(
            jnp.float32
        ) + kern_part[1, row].astype(jnp.float32)
    for slot, row in enumerate(order[:3]):
        for a in range(2):
            arrived(
                weights[a][1].at[:, span(row, lanes)],
                gw_send.at[a, 4 + slot],
                gw_recv.at[a, 4 + slot],
                {"rows": row},
            )
    for copy in started:
        copy.wait_send()


def finish_kernel(all_cols, nnz, in_mine, out_mine, in_grad, out_grad):
    block = in_grad.shape[2]
    for src, dst in ((in_mine, in_grad), (out_mine, out_grad)):
        for c in range(all_cols):
            for k in range(nnz):
                at = (c * nnz + k) * block
                dst[:, k * all_cols + c, :] = src[:, at : at + block].astype(jnp.float32)


def split_hidden(tokens, cotangent, weight_in, weight_out, mix_kernel, block_rows):
    n_rows, depth = lax.axis_size("rows"), lax.axis_size("hid")
    _, height, width, features = tokens.shape
    rows, all_cols, nnz, block = weight_in.shape
    count = height * width
    whole = count * n_rows
    model = features * depth
    cols = all_cols // n_rows
    lanes = cols * nnz * block
    hidden = cols * block
    bf16, f32 = jnp.bfloat16, jnp.float32
    dma, sds = pltpu.SemaphoreType.DMA, jax.ShapeDtypeStruct
    params = functools.partial(pltpu.CompilerParams, vmem_limit_bytes=60 * 1024 * 1024)
    tok_all, cot_all, in_all, out_all = pl.pallas_call(
        functools.partial(gather_kernel, depth),
        name="gather_parts",
        out_shape=[sds((whole, model), bf16)] * 2 + [sds((rows * n_rows, lanes), bf16)] * 2,
        in_specs=[ANY] * 4,
        out_specs=[ANY] * 4,
        scratch_shapes=[
            pltpu.VMEM((2, rows, nnz * all_cols, block), bf16),
            pltpu.VMEM((2, rows, all_cols * nnz * block), bf16),
            pltpu.VMEM((block // 128, rows * all_cols, 128), f32),
            dma((2, 4 * depth)),
            dma((2, n_rows, depth)),
            dma((2, 5)),
            dma((2, n_rows, 2)),
            dma((2, 2)),
            dma((2,)),
        ],
        compiler_params=params(collective_id=1, has_side_effects=True),
    )(
        tokens.reshape(count, features),
        cotangent.reshape(count, features),
        weight_in.transpose(0, 2, 1, 3).reshape(rows, nnz * all_cols, block),
        weight_out.transpose(0, 2, 1, 3).reshape(rows, nnz * all_cols, block),
    )
    dx, gw_in, gw_out, kern = pl.pallas_call(
        functools.partial(local_kernel, width, block, cols, nnz),
        name="local_math",
        out_shape=[
            sds((whole, model), bf16),
            sds((block, lanes), bf16),
            sds((block, lanes), bf16),
            sds((16, hidden), bf16),
        ],
        in_specs=[SMEM] + [VMEM] * 5,
        out_specs=[VMEM] * 4,
        scratch_shapes=[pltpu.VMEM((16, hidden), f32), pltpu.VMEM((whole, model), f32)]
        + [pltpu.VMEM((whole, block), f32)] * 4,
        compiler_params=params(),
    )(block_rows, tok_all, cot_all, in_all, out_all, mix_kernel)
    out_rows = block // (n_rows * lax.axis_size("crop"))
    dx_mine, in_mine, out_mine, kern_all = pl.pallas_call(
        functools.partial(scatter_kernel, depth),
        name="scatter_sums",
        out_shape=[
            sds((count, features), bf16),
            sds((out_rows, all_cols * nnz * block), bf16),
            sds((out_rows, all_cols * nnz * block), bf16),
            sds((16, hidden * n_rows), f32),
        ],
        in_specs=[VMEM] * 4,
        out_specs=[VMEM] * 4,
        scratch_shapes=[
            pltpu.VMEM((2, count, model), bf16),
            pltpu.VMEM((count, model), bf16),
            pltpu.VMEM((count, model), bf16),
            pltpu.VMEM((depth, count, features), bf16),
            pltpu.VMEM((depth - 1, count, features), bf16),
            pltpu.VMEM((2, 4, out_rows, lanes), bf16),
            pltpu.VMEM((2, 3, out_rows, lanes), bf16),
            pltpu.VMEM((2, n_rows, 16, hidden), bf16),
            dma((2 + depth,)),
            dma((2 + depth,)),
            dma((2, 7)),
            dma((2, 7)),
            dma((7,)),
            dma((2, n_rows)),
        ],
        compiler_params=params(collective_id=2, has_side_effects=True),
    )(dx, gw_in, gw_out, kern)
    step = 16
    flat_spec = pl.BlockSpec((step, all_cols * nnz * block), lambda i: (i, 0))
    grad_spec = pl.BlockSpec((step, nnz * all_cols, block), lambda i: (i, 0, 0))
    grads = pl.pallas_call(
        functools.partial(finish_kernel, all_cols, nnz),
        name="finish_weights",
        grid=(out_rows // step,),
        out_shape=[sds((out_rows, nnz * all_cols, block), f32)] * 2,
        in_specs=[flat_spec] * 2,
        out_specs=[grad_spec] * 2,
        compiler_params=params(),
    )(in_mine, out_mine)
    in_grad, out_grad = [
        grad.reshape(out_rows, nnz, all_cols, block).transpose(0, 2, 1, 3) for grad in grads
    ]
    return (dx_mine.reshape(tokens.shape), in_grad, out_grad, kern_all[: mix_kernel.shape[0]])


def padded(shard, sides, width):
    for axis, dim in sides:
        devices, length = (lax.axis_size(axis), shard.shape[dim])
        up = [(i, (i + 1) % devices) for i in range(devices - 1)]
        down = [(j, i) for i, j in up]
        last = lax.slice_in_dim(shard, length - width, length, axis=dim)
        initial = lax.slice_in_dim(shard, 0, width, axis=dim)
        before = lax.ppermute(last, axis, up)
        after = lax.ppermute(initial, axis, down)
        shard = jnp.concatenate([before, shard, after], axis=dim)
    return shard


def gelu_pair(preact):
    inner = root_two_pi * (preact + cubic_coef * preact * preact * preact)
    tanh_val = jnp.tanh(inner)
    gelu_out = 0.5 * preact * (1.0 + tanh_val)
    slopes = 0.5 * (1.0 + tanh_val) + 0.5 * preact * (1.0 - tanh_val * tanh_val) * root_two_pi * (
        1.0 + 3.0 * cubic_coef * preact * preact
    )
    return (gelu_out, slopes)


def on_device(tokens, cotangent, weight_in, weight_out, mix_kernel, block_rows):
    in_panel, out_panel = (
        lax.all_gather(weight_in, "rows", axis=0, tiled=True),
        lax.all_gather(weight_out, "rows", axis=0, tiled=True),
    )
    tok_full, cot_full = (
        lax.all_gather(tokens, "hid", axis=3, tiled=True),
        lax.all_gather(cotangent, "hid", axis=3, tiled=True),
    )
    crop_count, height, grid_width, depth_all = tok_full.shape
    tok_count = crop_count * height * grid_width
    block_size = in_panel.shape[0]
    col_count = in_panel.shape[1]
    nnz_count = in_panel.shape[2]
    block_count = depth_all // block_size
    hidden_local = col_count * block_size
    flat_rows = block_rows.reshape(-1)
    in_select = jnp.take(
        tok_full.reshape(tok_count, block_count, block_size), flat_rows, axis=1
    ).reshape(tok_count, col_count, nnz_count, block_size)
    grad_select = jnp.take(
        cot_full.reshape(tok_count, block_count, block_size), flat_rows, axis=1
    ).reshape(tok_count, col_count, nnz_count, block_size)
    pre_act = jnp.einsum("tckb,bcke->tce", in_select, in_panel, preferred_element_type=jnp.float32)
    gelu_out, slopes = gelu_pair(pre_act)
    active = gelu_out.astype(jnp.bfloat16).reshape(crop_count, height, grid_width, hidden_local)
    act_rim = padded(active, (("rows", 1),), 1)
    mix_grad = (
        jnp.einsum("tckd,fckd->tcf", grad_select, out_panel, preferred_element_type=jnp.float32)
        .astype(jnp.bfloat16)
        .reshape(crop_count, height, grid_width, hidden_local)
    )
    grad_rim = padded(mix_grad, (("rows", 1),), 1)
    act_pad = jnp.pad(act_rim.astype(jnp.float32), ((0, 0), (0, 0), (1, 1), (0, 0)))
    grad_pad = jnp.pad(grad_rim.astype(jnp.float32), ((0, 0), (0, 0), (1, 1), (0, 0)))
    grad_grid = mix_grad.astype(jnp.float32)
    mix_sum = jnp.zeros((crop_count, height, grid_width, hidden_local), jnp.float32)
    act_grad = jnp.zeros((crop_count, height, grid_width, hidden_local), jnp.float32)
    kern_terms = []
    for row_off in range(3):
        for col_off in range(3):
            tap = mix_kernel[3 * row_off + col_off]
            shifted = act_pad[:, row_off : row_off + height, col_off : col_off + grid_width]
            mix_sum = mix_sum + tap * shifted
            act_grad = (
                act_grad
                + tap
                * grad_pad[
                    :, 2 - row_off : 2 - row_off + height, 2 - col_off : 2 - col_off + grid_width
                ]
            )
            kern_terms.append(jnp.sum(shifted * grad_grid, axis=(0, 1, 2)))
    kern_local = jnp.stack(kern_terms, axis=0) * loss_scale
    mix_out = mix_sum.astype(jnp.bfloat16).reshape(tok_count, col_count, block_size)
    pre_grad = (act_grad.reshape(tok_count, col_count, block_size) * slopes).astype(jnp.bfloat16)
    kern_total = lax.psum(kern_local.astype(jnp.bfloat16), ("crop", "rows")).astype(jnp.float32)
    back_select = jnp.einsum(
        "tce,bcke->tckb", pre_grad, in_panel, preferred_element_type=jnp.float32
    )
    one_hot = (
        block_rows[:, :, None] == jnp.arange(block_count, dtype=jnp.int32)[None, None, :]
    ).astype(jnp.float32)
    token_terms = jnp.einsum(
        "tckb,ckr->trb", back_select, one_hot, precision=lax.Precision.HIGHEST
    ).reshape(crop_count, height, grid_width, depth_all)
    grad_tokens = lax.psum_scatter(
        token_terms.astype(jnp.bfloat16), "hid", scatter_dimension=3, tiled=True
    )
    first_term = jnp.einsum(
        "tckb,tce->bcke", in_select, pre_grad, preferred_element_type=jnp.float32
    )
    second_term = jnp.einsum(
        "tcf,tckd->fckd", mix_out, grad_select, preferred_element_type=jnp.float32
    )
    share_sums = lax.psum_scatter(
        (jnp.stack([first_term, second_term], axis=1) * loss_scale).astype(jnp.bfloat16),
        ("crop", "rows"),
        scatter_dimension=0,
        tiled=True,
    ).astype(jnp.float32)
    return (grad_tokens, share_sums[:, 0], share_sums[:, 1], kern_total)


def solution(mesh):
    placed = (
        P("crop", "rows", None, "hid"),
        P("crop", "rows", None, "hid"),
        P("rows", "hid", None, None),
        P("rows", "hid", None, None),
        P(None, "hid"),
        P("hid", None),
    )
    n_crop, n_rows = mesh.shape["crop"], mesh.shape["rows"]
    n_hid = mesh.shape["hid"]

    def step(tokens, cotangent, weight_in, weight_out, mix_kernel, block_rows):
        fits = (
            n_crop == 2
            and n_rows == 4
            and tokens.shape[0] == 1
            and weight_in.shape[1] % n_rows == 0
            and tokens.shape[1] * tokens.shape[2] * n_rows * tokens.shape[3] * n_hid <= 2**22
        )
        chosen = split_hidden if fits else on_device
        return chosen(tokens, cotangent, weight_in, weight_out, mix_kernel, block_rows)

    return jax.shard_map(
        step,
        mesh=mesh,
        in_specs=placed,
        out_specs=(
            P("crop", "rows", None, "hid"),
            P(("crop", "rows"), "hid", None, None),
            P(("crop", "rows"), "hid", None, None),
            P(None, "hid"),
        ),
        check_vma=False,
    )
```

```python
import functools

import jax
import jax.numpy as jnp
from jax import lax
from jax.experimental import pallas as pl
from jax.experimental.pallas import tpu as pltpu
from jax.sharding import PartitionSpec as P

root_two_pi = 0.7978845608
cubic_coef = 0.044715
loss_scale = 0.03125

MESH_ID = pl.DeviceIdType.MESH
ANY = pl.BlockSpec(memory_space=pl.ANY)
VMEM = pl.BlockSpec(memory_space=pltpu.VMEM)
SMEM = pl.BlockSpec(memory_space=pltpu.SMEM)


def span(start, size):
    return pl.ds(pl.multiple_of(start * size, size), size)


def neighbours():
    y, r, z = lax.axis_index("crop"), lax.axis_index("rows"), lax.axis_index("hid")
    x, core = r // 2, r % 2
    same_chip = x * 2 + (1 - core)
    across = (1 - x) * 2 + core
    diagonal = (1 - x) * 2 + (1 - core)
    return y, r, z, same_chip, across, diagonal


def enter(partners):
    barrier = pltpu.get_barrier_semaphore()
    for partner in partners:
        pl.semaphore_signal(barrier, inc=1, device_id=partner, device_id_type=MESH_ID)
    pl.semaphore_wait(barrier, len(partners))


def remote(src, dst, send_sem, recv_sem, target):
    return pltpu.make_async_remote_copy(
        src_ref=src,
        dst_ref=dst,
        send_sem=send_sem,
        recv_sem=recv_sem,
        device_id=target,
        device_id_type=MESH_ID,
    )


def gather_kernel(
    depth, tok, cot, w_in, w_out, tok_all, cot_all, in_all, out_all,
    raw, flat, stage, tok_send, tok_recv, w_send, w_recv, own_sem, raw_sem,
):
    y, r, z, same_chip, across, diagonal = neighbours()
    tokens, features = tok.shape
    rows = w_in.shape[0]
    lanes = in_all.shape[1]
    half = rows // 2
    block = w_in.shape[2]
    all_cols = stage.shape[1] // rows
    nnz = w_in.shape[1] // all_cols
    loads = [
        pltpu.make_async_copy(src, raw.at[a], raw_sem.at[a]) for a, src in enumerate((w_in, w_out))
    ]
    for load in loads:
        load.start()
    enter(
        [{"rows": same_chip}, {"rows": across}, {"rows": diagonal}, {"crop": 1 - y}]
        + [{"hid": (z + step) % depth} for step in range(1, depth)]
    )
    streams = ((tok, tok_all), (cot, cot_all))
    panels = ((flat.at[0], in_all), (flat.at[1], out_all))
    targets = ({"hid": z + 1}, {"hid": z - 1}, {"rows": across}, {"rows": same_chip})
    has_up, has_down = z + 1 < depth, z >= 1
    sends, local = [], []

    def launch(make, have=None):
        sends.append((make, have))
        if have is None:
            make().start()
        else:
            pl.when(have)(lambda: make().start())

    def piece(full, row, col):
        return full.at[span(row, tokens), span(col, features)]

    def pass_on(a, which, col, kind, have=None, own=False):
        def make():
            row = (r, across)[which]
            part = piece(streams[a][1], row, col)
            return remote(
                streams[a][0] if own else part,
                part,
                tok_send.at[a, which, col, kind],
                tok_recv.at[a, row, col],
                targets[kind],
            )

        launch(make, have)

    def await_piece(a, row, col, have=None):
        def wait():
            part = piece(streams[a][1], row, col)
            remote(
                part, part, tok_send.at[a, 0, 0, 3], tok_recv.at[a, row, col], {"rows": same_chip}
            ).wait_recv()

        if have is None:
            wait()
        else:
            pl.when(have)(wait)

    def half_rows(full, row, h):
        return full.at[pl.ds(pl.multiple_of(row * rows + h * half, half), half), :]

    def flatten(a):
        def turn(k, carry):
            for h in range(block // 128):
                part = raw[a, :, span(k, all_cols), h * 128 : (h + 1) * 128]
                stage[h] = part.astype(jnp.float32).reshape(rows * all_cols, 128)
            for c in range(all_cols):
                for h in range(block // 128):
                    flat[a, :, pl.ds(pl.multiple_of((c * nnz + k) * block + h * 128, 128), 128)] = stage[
                        h, pl.ds(c, rows, stride=all_cols), :
                    ].astype(jnp.bfloat16)
            return carry

        lax.fori_loop(0, nnz, turn, 0)

    def give_weights(a):
        src, full = panels[a]
        loads[a].wait()
        flatten(a)
        for slot, dest in ((1, across), (2, diagonal)):
            launch(
                lambda slot=slot, dest=dest: remote(
                    src.at[span(y, half), span(dest, lanes)],
                    half_rows(full, r, y),
                    w_send.at[a, slot],
                    w_recv.at[a, r, y],
                    {"rows": dest},
                )
            )
        launch(
            lambda: remote(
                src.at[:, span(same_chip, lanes)],
                full.at[span(r, rows), :],
                w_send.at[a, 0],
                w_recv.at[a, r, 0],
                {"rows": same_chip},
            )
        )
        keep = pltpu.make_async_copy(
            src.at[:, span(r, lanes)], full.at[span(r, rows), :], own_sem.at[a, 1]
        )
        keep.start()
        local.append(keep)

    def mirror_weights(a):
        full = panels[a][1]
        for slot, row in ((3, across), (4, diagonal)):
            part = half_rows(full, row, y)
            remote(part, part, w_send.at[a, slot], w_recv.at[a, row, y], {"rows": row}).wait_recv()
            launch(
                lambda slot=slot, row=row, part=part: remote(
                    part, part, w_send.at[a, slot], w_recv.at[a, row, y], {"crop": 1 - y}
                )
            )

    def line_step(step):
        for below in (True, False):
            col = z - step if below else z + step
            have = col >= 0 if below else col < depth
            onward = jnp.logical_and(have, has_up if below else has_down)
            for a, which in ((0, 0), (1, 0), (1, 1)):
                await_piece(a, (r, across)[which], col, have)
                pass_on(a, which, col, 0 if below else 1, onward)
                if a == 0:
                    pass_on(a, which, col, 2, have)
                pass_on(a, which, col, 3, have)

    for a, kind in ((1, 2), (0, 0), (0, 1), (1, 0), (1, 1), (0, 2), (0, 3), (1, 3)):
        pass_on(a, 0, z, kind, (has_up, has_down, None, None)[kind], own=True)
    for a in range(2):
        keep = pltpu.make_async_copy(streams[a][0], piece(streams[a][1], r, z), own_sem.at[a, 0])
        keep.start()
        local.append(keep)
    give_weights(0)
    await_piece(1, across, z)
    for kind in (0, 1, 3):
        pass_on(1, 1, z, kind, (has_up, has_down, None, None)[kind])
    give_weights(1)
    for step in range(1, depth - 1):
        line_step(step)
    for a in range(2):
        mirror_weights(a)
    line_step(depth - 1)
    for step in range(depth):
        col = (z + step) % depth
        await_piece(0, across, col)
        pass_on(0, 1, col, 3)
    for a in range(2):
        full = panels[a][1]
        part = full.at[span(same_chip, rows), :]
        remote(
            part, part, w_send.at[a, 0], w_recv.at[a, same_chip, 0], {"rows": same_chip}
        ).wait_recv()
        for row in (across, diagonal):
            part = half_rows(full, row, 1 - y)
            remote(
                part, part, w_send.at[a, 0], w_recv.at[a, row, 1 - y], {"crop": 1 - y}
            ).wait_recv()
        for row in (same_chip, diagonal):
            for step in range(depth):
                await_piece(a, row, (z + step) % depth)
    for copy in local:
        copy.wait()
    for make, have in sends:
        if have is None:
            make().wait_send()
        else:
            pl.when(have)(lambda make=make: make().wait_send())


def nt(a, b):
    return lax.dot_general(a, b, (((1,), (1,)), ((), ())), preferred_element_type=jnp.float32)


def tn(a, b):
    return lax.dot_general(a, b, (((0,), (0,)), ((), ())), preferred_element_type=jnp.float32)


def local_kernel(
    width, block, cols, nnz, ids, tok, cot, w_in, w_out, taps,
    dx_out, gw_in, gw_out, kern_out, kern, dx, pre_s, act_s, slope_s, mg_s,
):
    count = tok.shape[0]
    me = lax.axis_index("rows")
    dx[...] = jnp.zeros_like(dx)
    place = lax.broadcasted_iota(jnp.int32, (count, block), 0) % width
    kern[...] = jnp.zeros_like(kern)

    def spread(value):
        before = jnp.where(place == 0, 0.0, pltpu.roll(value, 1, 0))
        after = jnp.where(place == width - 1, 0.0, pltpu.roll(value, count - 1, 0))
        return (before, value, after)

    def stack_rows(up, mid, down):
        edge = jnp.zeros((width, block), jnp.float32)
        return (
            mid
            + jnp.concatenate([edge, up[:-width]], axis=0)
            + jnp.concatenate([down[width:], edge], axis=0)
        )

    def column(c, carry):
        hidden = span(c, block)

        def feats(k):
            return span(ids[me * cols + c, k], block)

        def panel(k):
            return span(c * nnz + k, block)

        pre = jnp.dot(tok[:, feats(0)], w_in[:, panel(0)], preferred_element_type=jnp.float32)
        for k in range(1, nnz):
            pre += jnp.dot(tok[:, feats(k)], w_in[:, panel(k)], preferred_element_type=jnp.float32)
        pre_s[...] = pre
        mg = nt(cot[:, feats(0)], w_out[:, panel(0)])
        for k in range(1, nnz):
            mg += nt(cot[:, feats(k)], w_out[:, panel(k)])
        mg_s[...] = mg.astype(jnp.bfloat16).astype(jnp.float32)
        p = pre_s[...]
        t = jnp.tanh(root_two_pi * (p + cubic_coef * p * p * p))
        act_s[...] = (0.5 * p * (1.0 + t)).astype(jnp.bfloat16).astype(jnp.float32)
        slope_s[...] = 0.5 * (1.0 + t) + 0.5 * p * (1.0 - t * t) * root_two_pi * (
            1.0 + 3.0 * cubic_coef * p * p
        )

        def tap(a, b):
            row = 3 * (a + 1) + (b + 1)
            return taps[row : row + 1, span(me * cols + c, block)]

        acts = spread(act_s[...])
        mixed = stack_rows(
            *[sum(tap(a, b) * acts[b + 1] for b in (-1, 0, 1)) for a in (-1, 0, 1)]
        ).astype(jnp.bfloat16)
        grads = mg_s[...]
        for b in (-1, 0, 1):
            seen = acts[b + 1]
            sums = (
                jnp.sum(seen[:-width] * grads[width:], axis=0, keepdims=True),
                jnp.sum(seen * grads, axis=0, keepdims=True),
                jnp.sum(seen[width:] * grads[:-width], axis=0, keepdims=True),
            )
            for a in (-1, 0, 1):
                row = 3 * (a + 1) + (b + 1)
                kern[row : row + 1, hidden] = sums[a + 1] * loss_scale
        for k in range(nnz):
            gw_out[:, panel(k)] = (tn(mixed, cot[:, feats(k)]) * loss_scale).astype(jnp.bfloat16)
        backs = spread(mg_s[...])
        gathered = stack_rows(
            *[sum(tap(a, b) * backs[1 - b] for b in (-1, 0, 1)) for a in (1, 0, -1)]
        )
        pre_grad = (gathered * slope_s[...]).astype(jnp.bfloat16)
        for k in range(nnz):
            gw_in[:, panel(k)] = (tn(tok[:, feats(k)], pre_grad) * loss_scale).astype(jnp.bfloat16)
            dx[:, feats(k)] += nt(pre_grad, w_in[:, panel(k)])
        return carry

    lax.fori_loop(0, cols, column, 0)
    dx_out[...] = dx[...].astype(jnp.bfloat16)
    kern_out[...] = kern[...].astype(jnp.bfloat16)


def scatter_kernel(
    depth, dx, gw_in, gw_out, kern, dx_mine, in_mine, out_mine, kern_all,
    dx_near, dx_half, dx_far, dx_sum, dx_last, gw_part, gw_sum, kern_part,
    dx_send, dx_recv, gw_send, gw_recv, kern_send, kern_recv,
):
    y, r, z, same_chip, across, diagonal = neighbours()
    group = [same_chip, across, diagonal]
    enter(
        [{"rows": row} for row in group]
        + [{"crop": 1 - y, "rows": row} for row in group]
        + [{"crop": 1 - y}]
        + [{"hid": (z + step) % depth} for step in range(1, depth)]
    )
    started = []

    def go(*args):
        copy = remote(*args)
        copy.start()
        started.append(copy)

    tokens, features = dx_mine.shape
    rows = in_mine.shape[0]
    lanes = gw_in.shape[1]
    weights = ((gw_in, in_mine), (gw_out, out_mine))
    for slot, row in enumerate((diagonal, same_chip)):
        go(dx.at[span(row, tokens), :], dx_near.at[slot], dx_send.at[slot], dx_recv.at[slot], {"rows": same_chip})
    order = (across, diagonal, same_chip, r)
    for slot, row in enumerate(order):
        for a in range(2):
            go(
                weights[a][0].at[span((1 - y) * 4 + row, rows), :],
                gw_part.at[a, slot],
                gw_send.at[a, slot],
                gw_recv.at[a, slot],
                {"crop": 1 - y},
            )
    for slot, row in enumerate(group):
        go(kern, kern_part.at[y, r], kern_send.at[slot], kern_recv.at[y, r], {"rows": row})
        go(
            kern,
            kern_part.at[y, r],
            kern_send.at[slot + 3],
            kern_recv.at[y, r],
            {"crop": 1 - y, "rows": row},
        )
    go(kern, kern_part.at[y, r], kern_send.at[6], kern_recv.at[y, r], {"crop": 1 - y})

    def arrived(ref, send_sem, recv_sem, target):
        remote(ref, ref, send_sem, recv_sem, target).wait_recv()

    arrived(dx_near.at[0], dx_send.at[0], dx_recv.at[0], {"rows": same_chip})
    dx_half[...] = (
        dx[span(across, tokens), :].astype(jnp.float32) + dx_near[0].astype(jnp.float32)
    ).astype(jnp.bfloat16)
    go(dx_half, dx_far, dx_send.at[2], dx_recv.at[2], {"rows": across})
    arrived(dx_near.at[1], dx_send.at[1], dx_recv.at[1], {"rows": same_chip})
    arrived(dx_far, dx_send.at[2], dx_recv.at[2], {"rows": across})
    for col in range(depth):
        part = slice(col * features, (col + 1) * features)
        dx_sum[col] = (
            dx[span(r, tokens), part].astype(jnp.float32)
            + dx_near[1, :, part].astype(jnp.float32)
            + dx_far[:, part].astype(jnp.float32)
        ).astype(jnp.bfloat16)
    for step in range(1, depth):
        go(
            dx_sum.at[(z + step) % depth],
            dx_last.at[step - 1],
            dx_send.at[2 + step],
            dx_recv.at[2 + step],
            {"hid": (z + step) % depth},
        )
    for slot, row in enumerate(order):
        for a in range(2):
            arrived(gw_part.at[a, slot], gw_send.at[a, slot], gw_recv.at[a, slot], {"crop": 1 - y})
            total = (
                weights[a][0][span(y * 4 + row, rows), :].astype(jnp.float32)
                + gw_part[a, slot].astype(jnp.float32)
            ).astype(jnp.bfloat16)
            if slot == 3:
                weights[a][1][:, span(r, lanes)] = total
            else:
                gw_sum[a, slot] = total
                go(
                    gw_sum.at[a, slot],
                    weights[a][1].at[:, span(r, lanes)],
                    gw_send.at[a, 4 + slot],
                    gw_recv.at[a, 4 + slot],
                    {"rows": row},
                )
    total = dx_sum[z].astype(jnp.float32)
    for step in range(1, depth):
        arrived(dx_last.at[step - 1], dx_send.at[2 + step], dx_recv.at[2 + step], {"hid": (z + step) % depth})
        total += dx_last[step - 1].astype(jnp.float32)
    dx_mine[...] = total.astype(jnp.bfloat16)
    kern_part[y, r] = kern[...]
    for row in group:
        for crop in (y, 1 - y):
            arrived(kern_part.at[crop, row], kern_send.at[0], kern_recv.at[crop, row], {"rows": same_chip})
    arrived(kern_part.at[1 - y, r], kern_send.at[0], kern_recv.at[1 - y, r], {"rows": same_chip})
    wide = kern.shape[1]
    for row in range(4):
        kern_all[:, row * wide : (row + 1) * wide] = kern_part[0, row].astype(
            jnp.float32
        ) + kern_part[1, row].astype(jnp.float32)
    for slot, row in enumerate(order[:3]):
        for a in range(2):
            arrived(
                weights[a][1].at[:, span(row, lanes)],
                gw_send.at[a, 4 + slot],
                gw_recv.at[a, 4 + slot],
                {"rows": row},
            )
    for copy in started:
        copy.wait_send()


def finish_kernel(all_cols, nnz, in_mine, out_mine, in_grad, out_grad):
    block = in_grad.shape[2]
    for src, dst in ((in_mine, in_grad), (out_mine, out_grad)):
        for c in range(all_cols):
            for k in range(nnz):
                at = (c * nnz + k) * block
                dst[:, k * all_cols + c, :] = src[:, at : at + block].astype(jnp.float32)


def split_hidden(tokens, cotangent, weight_in, weight_out, mix_kernel, block_rows):
    n_rows, depth = lax.axis_size("rows"), lax.axis_size("hid")
    _, height, width, features = tokens.shape
    rows, all_cols, nnz, block = weight_in.shape
    count = height * width
    whole = count * n_rows
    model = features * depth
    cols = all_cols // n_rows
    lanes = cols * nnz * block
    hidden = cols * block
    bf16, f32 = jnp.bfloat16, jnp.float32
    dma, sds = pltpu.SemaphoreType.DMA, jax.ShapeDtypeStruct
    params = functools.partial(pltpu.CompilerParams, vmem_limit_bytes=60 * 1024 * 1024)
    tok_all, cot_all, in_all, out_all = pl.pallas_call(
        functools.partial(gather_kernel, depth),
        name="gather_parts",
        out_shape=[sds((whole, model), bf16)] * 2 + [sds((rows * n_rows, lanes), bf16)] * 2,
        in_specs=[ANY] * 4,
        out_specs=[ANY] * 4,
        scratch_shapes=[
            pltpu.VMEM((2, rows, nnz * all_cols, block), bf16),
            pltpu.VMEM((2, rows, all_cols * nnz * block), bf16),
            pltpu.VMEM((block // 128, rows * all_cols, 128), f32),
            dma((2, 2, depth, 4)),
            dma((2, n_rows, depth)),
            dma((2, 5)),
            dma((2, n_rows, 2)),
            dma((2, 2)),
            dma((2,)),
        ],
        compiler_params=params(collective_id=1, has_side_effects=True),
    )(
        tokens.reshape(count, features),
        cotangent.reshape(count, features),
        weight_in.transpose(0, 2, 1, 3).reshape(rows, nnz * all_cols, block),
        weight_out.transpose(0, 2, 1, 3).reshape(rows, nnz * all_cols, block),
    )
    dx, gw_in, gw_out, kern = pl.pallas_call(
        functools.partial(local_kernel, width, block, cols, nnz),
        name="local_math",
        out_shape=[
            sds((whole, model), bf16),
            sds((block, lanes), bf16),
            sds((block, lanes), bf16),
            sds((16, hidden), bf16),
        ],
        in_specs=[SMEM] + [VMEM] * 5,
        out_specs=[VMEM] * 4,
        scratch_shapes=[pltpu.VMEM((16, hidden), f32), pltpu.VMEM((whole, model), f32)]
        + [pltpu.VMEM((whole, block), f32)] * 4,
        compiler_params=params(),
    )(block_rows, tok_all, cot_all, in_all, out_all, mix_kernel)
    out_rows = block // (n_rows * lax.axis_size("crop"))
    dx_mine, in_mine, out_mine, kern_all = pl.pallas_call(
        functools.partial(scatter_kernel, depth),
        name="scatter_sums",
        out_shape=[
            sds((count, features), bf16),
            sds((out_rows, all_cols * nnz * block), bf16),
            sds((out_rows, all_cols * nnz * block), bf16),
            sds((16, hidden * n_rows), f32),
        ],
        in_specs=[VMEM] * 4,
        out_specs=[VMEM] * 4,
        scratch_shapes=[
            pltpu.VMEM((2, count, model), bf16),
            pltpu.VMEM((count, model), bf16),
            pltpu.VMEM((count, model), bf16),
            pltpu.VMEM((depth, count, features), bf16),
            pltpu.VMEM((depth - 1, count, features), bf16),
            pltpu.VMEM((2, 4, out_rows, lanes), bf16),
            pltpu.VMEM((2, 3, out_rows, lanes), bf16),
            pltpu.VMEM((2, n_rows, 16, hidden), bf16),
            dma((2 + depth,)),
            dma((2 + depth,)),
            dma((2, 7)),
            dma((2, 7)),
            dma((7,)),
            dma((2, n_rows)),
        ],
        compiler_params=params(collective_id=2, has_side_effects=True),
    )(dx, gw_in, gw_out, kern)
    step = 16
    flat_spec = pl.BlockSpec((step, all_cols * nnz * block), lambda i: (i, 0))
    grad_spec = pl.BlockSpec((step, nnz * all_cols, block), lambda i: (i, 0, 0))
    grads = pl.pallas_call(
        functools.partial(finish_kernel, all_cols, nnz),
        name="finish_weights",
        grid=(out_rows // step,),
        out_shape=[sds((out_rows, nnz * all_cols, block), f32)] * 2,
        in_specs=[flat_spec] * 2,
        out_specs=[grad_spec] * 2,
        compiler_params=params(),
    )(in_mine, out_mine)
    in_grad, out_grad = [
        grad.reshape(out_rows, nnz, all_cols, block).transpose(0, 2, 1, 3) for grad in grads
    ]
    return (dx_mine.reshape(tokens.shape), in_grad, out_grad, kern_all[: mix_kernel.shape[0]])


def padded(shard, sides, width):
    for axis, dim in sides:
        devices, length = (lax.axis_size(axis), shard.shape[dim])
        up = [(i, (i + 1) % devices) for i in range(devices - 1)]
        down = [(j, i) for i, j in up]
        last = lax.slice_in_dim(shard, length - width, length, axis=dim)
        initial = lax.slice_in_dim(shard, 0, width, axis=dim)
        before = lax.ppermute(last, axis, up)
        after = lax.ppermute(initial, axis, down)
        shard = jnp.concatenate([before, shard, after], axis=dim)
    return shard


def gelu_pair(preact):
    inner = root_two_pi * (preact + cubic_coef * preact * preact * preact)
    tanh_val = jnp.tanh(inner)
    gelu_out = 0.5 * preact * (1.0 + tanh_val)
    slopes = 0.5 * (1.0 + tanh_val) + 0.5 * preact * (1.0 - tanh_val * tanh_val) * root_two_pi * (
        1.0 + 3.0 * cubic_coef * preact * preact
    )
    return (gelu_out, slopes)


def on_device(tokens, cotangent, weight_in, weight_out, mix_kernel, block_rows):
    in_panel, out_panel = (
        lax.all_gather(weight_in, "rows", axis=0, tiled=True),
        lax.all_gather(weight_out, "rows", axis=0, tiled=True),
    )
    tok_full, cot_full = (
        lax.all_gather(tokens, "hid", axis=3, tiled=True),
        lax.all_gather(cotangent, "hid", axis=3, tiled=True),
    )
    crop_count, height, grid_width, depth_all = tok_full.shape
    tok_count = crop_count * height * grid_width
    block_size = in_panel.shape[0]
    col_count = in_panel.shape[1]
    nnz_count = in_panel.shape[2]
    block_count = depth_all // block_size
    hidden_local = col_count * block_size
    flat_rows = block_rows.reshape(-1)
    in_select = jnp.take(
        tok_full.reshape(tok_count, block_count, block_size), flat_rows, axis=1
    ).reshape(tok_count, col_count, nnz_count, block_size)
    grad_select = jnp.take(
        cot_full.reshape(tok_count, block_count, block_size), flat_rows, axis=1
    ).reshape(tok_count, col_count, nnz_count, block_size)
    pre_act = jnp.einsum("tckb,bcke->tce", in_select, in_panel, preferred_element_type=jnp.float32)
    gelu_out, slopes = gelu_pair(pre_act)
    active = gelu_out.astype(jnp.bfloat16).reshape(crop_count, height, grid_width, hidden_local)
    act_rim = padded(active, (("rows", 1),), 1)
    mix_grad = (
        jnp.einsum("tckd,fckd->tcf", grad_select, out_panel, preferred_element_type=jnp.float32)
        .astype(jnp.bfloat16)
        .reshape(crop_count, height, grid_width, hidden_local)
    )
    grad_rim = padded(mix_grad, (("rows", 1),), 1)
    act_pad = jnp.pad(act_rim.astype(jnp.float32), ((0, 0), (0, 0), (1, 1), (0, 0)))
    grad_pad = jnp.pad(grad_rim.astype(jnp.float32), ((0, 0), (0, 0), (1, 1), (0, 0)))
    grad_grid = mix_grad.astype(jnp.float32)
    mix_sum = jnp.zeros((crop_count, height, grid_width, hidden_local), jnp.float32)
    act_grad = jnp.zeros((crop_count, height, grid_width, hidden_local), jnp.float32)
    kern_terms = []
    for row_off in range(3):
        for col_off in range(3):
            tap = mix_kernel[3 * row_off + col_off]
            shifted = act_pad[:, row_off : row_off + height, col_off : col_off + grid_width]
            mix_sum = mix_sum + tap * shifted
            act_grad = (
                act_grad
                + tap
                * grad_pad[
                    :, 2 - row_off : 2 - row_off + height, 2 - col_off : 2 - col_off + grid_width
                ]
            )
            kern_terms.append(jnp.sum(shifted * grad_grid, axis=(0, 1, 2)))
    kern_local = jnp.stack(kern_terms, axis=0) * loss_scale
    mix_out = mix_sum.astype(jnp.bfloat16).reshape(tok_count, col_count, block_size)
    pre_grad = (act_grad.reshape(tok_count, col_count, block_size) * slopes).astype(jnp.bfloat16)
    kern_total = lax.psum(kern_local.astype(jnp.bfloat16), ("crop", "rows")).astype(jnp.float32)
    back_select = jnp.einsum(
        "tce,bcke->tckb", pre_grad, in_panel, preferred_element_type=jnp.float32
    )
    one_hot = (
        block_rows[:, :, None] == jnp.arange(block_count, dtype=jnp.int32)[None, None, :]
    ).astype(jnp.float32)
    token_terms = jnp.einsum(
        "tckb,ckr->trb", back_select, one_hot, precision=lax.Precision.HIGHEST
    ).reshape(crop_count, height, grid_width, depth_all)
    grad_tokens = lax.psum_scatter(
        token_terms.astype(jnp.bfloat16), "hid", scatter_dimension=3, tiled=True
    )
    first_term = jnp.einsum(
        "tckb,tce->bcke", in_select, pre_grad, preferred_element_type=jnp.float32
    )
    second_term = jnp.einsum(
        "tcf,tckd->fckd", mix_out, grad_select, preferred_element_type=jnp.float32
    )
    share_sums = lax.psum_scatter(
        (jnp.stack([first_term, second_term], axis=1) * loss_scale).astype(jnp.bfloat16),
        ("crop", "rows"),
        scatter_dimension=0,
        tiled=True,
    ).astype(jnp.float32)
    return (grad_tokens, share_sums[:, 0], share_sums[:, 1], kern_total)


def solution(mesh):
    placed = (
        P("crop", "rows", None, "hid"),
        P("crop", "rows", None, "hid"),
        P("rows", "hid", None, None),
        P("rows", "hid", None, None),
        P(None, "hid"),
        P("hid", None),
    )
    n_crop, n_rows = mesh.shape["crop"], mesh.shape["rows"]
    n_hid = mesh.shape["hid"]

    def step(tokens, cotangent, weight_in, weight_out, mix_kernel, block_rows):
        fits = (
            n_crop == 2
            and n_rows == 4
            and tokens.shape[0] == 1
            and weight_in.shape[1] % n_rows == 0
            and tokens.shape[1] * tokens.shape[2] * n_rows * tokens.shape[3] * n_hid <= 2**22
        )
        chosen = split_hidden if fits else on_device
        return chosen(tokens, cotangent, weight_in, weight_out, mix_kernel, block_rows)

    return jax.shard_map(
        step,
        mesh=mesh,
        in_specs=placed,
        out_specs=(
            P("crop", "rows", None, "hid"),
            P(("crop", "rows"), "hid", None, None),
            P(("crop", "rows"), "hid", None, None),
            P(None, "hid"),
        ),
        check_vma=False,
    )
```

```python
import functools

import jax
import jax.numpy as jnp
from jax import lax
from jax.experimental import pallas as pl
from jax.experimental.pallas import tpu as pltpu
from jax.sharding import PartitionSpec as P

root_two_pi = 0.7978845608
cubic_coef = 0.044715
loss_scale = 0.03125

MESH_ID = pl.DeviceIdType.MESH
ANY = pl.BlockSpec(memory_space=pl.ANY)
VMEM = pl.BlockSpec(memory_space=pltpu.VMEM)
SMEM = pl.BlockSpec(memory_space=pltpu.SMEM)


def span(start, size):
    return pl.ds(pl.multiple_of(start * size, size), size)


def neighbours():
    y, r, z = lax.axis_index("crop"), lax.axis_index("rows"), lax.axis_index("hid")
    x, core = r // 2, r % 2
    same_chip = x * 2 + (1 - core)
    across = (1 - x) * 2 + core
    diagonal = (1 - x) * 2 + (1 - core)
    return y, r, z, same_chip, across, diagonal


def enter(partners):
    barrier = pltpu.get_barrier_semaphore()
    for partner in partners:
        pl.semaphore_signal(barrier, inc=1, device_id=partner, device_id_type=MESH_ID)
    pl.semaphore_wait(barrier, len(partners))


def remote(src, dst, send_sem, recv_sem, target):
    return pltpu.make_async_remote_copy(
        src_ref=src,
        dst_ref=dst,
        send_sem=send_sem,
        recv_sem=recv_sem,
        device_id=target,
        device_id_type=MESH_ID,
    )


def gather_kernel(
    depth, tok, cot, w_in, w_out, tok_all, cot_all, in_all, out_all,
    raw, flat, stage, tok_send, tok_recv, w_send, w_recv, own_sem, raw_sem,
):
    y, r, z, same_chip, across, diagonal = neighbours()
    tokens, features = tok.shape
    rows = w_in.shape[0]
    lanes = in_all.shape[1]
    half = rows // 2
    block = w_in.shape[2]
    all_cols = stage.shape[1] // rows
    nnz = w_in.shape[1] // all_cols
    loads = [
        pltpu.make_async_copy(src, raw.at[a], raw_sem.at[a]) for a, src in enumerate((w_in, w_out))
    ]
    for load in loads:
        load.start()
    enter(
        [{"rows": same_chip}, {"rows": across}, {"rows": diagonal}, {"crop": 1 - y}]
        + [{"hid": (z + step) % depth} for step in range(1, depth)]
    )
    streams = ((tok, tok_all), (cot, cot_all))
    panels = ((flat.at[0], in_all), (flat.at[1], out_all))
    targets = ({"hid": z + 1}, {"hid": z - 1}, {"rows": across}, {"rows": same_chip})
    has_up, has_down = z + 1 < depth, z >= 1
    sends, local = [], []

    def launch(make, have=None):
        sends.append((make, have))
        if have is None:
            make().start()
        else:
            pl.when(have)(lambda: make().start())

    def piece(full, row, col):
        return full.at[span(row, tokens), span(col, features)]

    def pass_on(a, which, col, kind, have=None, own=False):
        def make():
            row = (r, across)[which]
            part = piece(streams[a][1], row, col)
            return remote(
                streams[a][0] if own else part,
                part,
                tok_send.at[a, which, col, kind],
                tok_recv.at[a, row, col],
                targets[kind],
            )

        launch(make, have)

    def await_piece(a, row, col, have=None):
        def wait():
            part = piece(streams[a][1], row, col)
            remote(
                part, part, tok_send.at[a, 0, 0, 3], tok_recv.at[a, row, col], {"rows": same_chip}
            ).wait_recv()

        if have is None:
            wait()
        else:
            pl.when(have)(wait)

    def half_rows(full, row, h):
        return full.at[pl.ds(pl.multiple_of(row * rows + h * half, half), half), :]

    def flatten(a):
        def turn(k, carry):
            for h in range(block // 128):
                part = raw[a, :, span(k, all_cols), h * 128 : (h + 1) * 128]
                stage[h] = part.astype(jnp.float32).reshape(rows * all_cols, 128)
            for c in range(all_cols):
                for h in range(block // 128):
                    flat[a, :, pl.ds(pl.multiple_of((c * nnz + k) * block + h * 128, 128), 128)] = stage[
                        h, pl.ds(c, rows, stride=all_cols), :
                    ].astype(jnp.bfloat16)
            return carry

        lax.fori_loop(0, nnz, turn, 0)

    def give_weights(a):
        src, full = panels[a]
        loads[a].wait()
        flatten(a)
        for slot, dest in ((1, across), (2, diagonal)):
            launch(
                lambda slot=slot, dest=dest: remote(
                    src.at[span(y, half), span(dest, lanes)],
                    half_rows(full, r, y),
                    w_send.at[a, slot],
                    w_recv.at[a, r, y],
                    {"rows": dest},
                )
            )
        launch(
            lambda: remote(
                src.at[:, span(same_chip, lanes)],
                full.at[span(r, rows), :],
                w_send.at[a, 0],
                w_recv.at[a, r, 0],
                {"rows": same_chip},
            )
        )
        keep = pltpu.make_async_copy(
            src.at[:, span(r, lanes)], full.at[span(r, rows), :], own_sem.at[a, 1]
        )
        keep.start()
        local.append(keep)

    def mirror_weights(a):
        full = panels[a][1]
        for slot, row in ((3, across), (4, diagonal)):
            part = half_rows(full, row, y)
            remote(part, part, w_send.at[a, slot], w_recv.at[a, row, y], {"rows": row}).wait_recv()
            launch(
                lambda slot=slot, row=row, part=part: remote(
                    part, part, w_send.at[a, slot], w_recv.at[a, row, y], {"crop": 1 - y}
                )
            )

    def line_step(step):
        for below in (True, False):
            col = z - step if below else z + step
            have = col >= 0 if below else col < depth
            onward = jnp.logical_and(have, has_up if below else has_down)
            for a, which in ((0, 0), (1, 0), (1, 1)):
                await_piece(a, (r, across)[which], col, have)
                pass_on(a, which, col, 0 if below else 1, onward)
                if a == 0:
                    pass_on(a, which, col, 2, have)
                pass_on(a, which, col, 3, have)

    for a, kind in ((1, 2), (0, 0), (0, 1), (1, 0), (1, 1), (0, 2), (0, 3), (1, 3)):
        pass_on(a, 0, z, kind, (has_up, has_down, None, None)[kind], own=True)
    for a in range(2):
        keep = pltpu.make_async_copy(streams[a][0], piece(streams[a][1], r, z), own_sem.at[a, 0])
        keep.start()
        local.append(keep)
    give_weights(0)
    await_piece(1, across, z)
    for kind in (0, 1, 3):
        pass_on(1, 1, z, kind, (has_up, has_down, None, None)[kind])
    give_weights(1)
    for step in range(1, depth - 1):
        line_step(step)
    for a in range(2):
        mirror_weights(a)
    line_step(depth - 1)
    for step in range(depth):
        col = (z + step) % depth
        await_piece(0, across, col)
        pass_on(0, 1, col, 3)
    for a in range(2):
        full = panels[a][1]
        part = full.at[span(same_chip, rows), :]
        remote(
            part, part, w_send.at[a, 0], w_recv.at[a, same_chip, 0], {"rows": same_chip}
        ).wait_recv()
        for row in (across, diagonal):
            part = half_rows(full, row, 1 - y)
            remote(
                part, part, w_send.at[a, 0], w_recv.at[a, row, 1 - y], {"crop": 1 - y}
            ).wait_recv()
        for row in (same_chip, diagonal):
            for step in range(depth):
                await_piece(a, row, (z + step) % depth)
    for copy in local:
        copy.wait()
    for make, have in sends:
        if have is None:
            make().wait_send()
        else:
            pl.when(have)(lambda make=make: make().wait_send())


def nt(a, b):
    return lax.dot_general(a, b, (((1,), (1,)), ((), ())), preferred_element_type=jnp.float32)


def tn(a, b):
    return lax.dot_general(a, b, (((0,), (0,)), ((), ())), preferred_element_type=jnp.float32)


def local_kernel(
    width, block, cols, nnz, ids, tok, cot, w_in, w_out, taps,
    dx_out, gw_in, gw_out, kern_out, kern, dx, pre_s, act_s, slope_s, mg_s,
):
    count = tok.shape[0]
    me = lax.axis_index("rows")
    c = pl.program_id(0)
    place = lax.broadcasted_iota(jnp.int32, (count, block), 0) % width

    @pl.when(c == 0)
    def _():
        dx[...] = jnp.zeros_like(dx)
        kern[...] = jnp.zeros_like(kern)

    def spread(value):
        before = jnp.where(place == 0, 0.0, pltpu.roll(value, 1, 0))
        after = jnp.where(place == width - 1, 0.0, pltpu.roll(value, count - 1, 0))
        return (before, value, after)

    def stack_rows(up, mid, down):
        edge = jnp.zeros((width, block), jnp.float32)
        return (
            mid
            + jnp.concatenate([edge, up[:-width]], axis=0)
            + jnp.concatenate([down[width:], edge], axis=0)
        )

    hidden = span(c, block)

    def feats(k):
        return span(ids[k, me * cols + c], block)

    def panel(k):
        return slice(k * block, (k + 1) * block)

    pre = jnp.dot(tok[:, feats(0)], w_in[:, panel(0)], preferred_element_type=jnp.float32)
    for k in range(1, nnz):
        pre += jnp.dot(tok[:, feats(k)], w_in[:, panel(k)], preferred_element_type=jnp.float32)
    pre_s[...] = pre
    mg = nt(cot[:, feats(0)], w_out[:, panel(0)])
    for k in range(1, nnz):
        mg += nt(cot[:, feats(k)], w_out[:, panel(k)])
    mg_s[...] = mg.astype(jnp.bfloat16).astype(jnp.float32)
    p = pre_s[...]
    t = jnp.tanh(root_two_pi * (p + cubic_coef * p * p * p))
    act_s[...] = (0.5 * p * (1.0 + t)).astype(jnp.bfloat16).astype(jnp.float32)
    slope_s[...] = 0.5 * (1.0 + t) + 0.5 * p * (1.0 - t * t) * root_two_pi * (
        1.0 + 3.0 * cubic_coef * p * p
    )

    def tap(a, b):
        row = 3 * (a + 1) + (b + 1)
        return taps[row : row + 1, span(me * cols + c, block)]

    acts = spread(act_s[...])
    mixed = stack_rows(
        *[sum(tap(a, b) * acts[b + 1] for b in (-1, 0, 1)) for a in (-1, 0, 1)]
    ).astype(jnp.bfloat16)
    grads = mg_s[...]
    for b in (-1, 0, 1):
        seen = acts[b + 1]
        sums = (
            jnp.sum(seen[:-width] * grads[width:], axis=0, keepdims=True),
            jnp.sum(seen * grads, axis=0, keepdims=True),
            jnp.sum(seen[width:] * grads[:-width], axis=0, keepdims=True),
        )
        for a in (-1, 0, 1):
            row = 3 * (a + 1) + (b + 1)
            kern[row : row + 1, hidden] = sums[a + 1] * loss_scale
    for k in range(nnz):
        gw_out[:, panel(k)] = (tn(mixed, cot[:, feats(k)]) * loss_scale).astype(jnp.bfloat16)
    backs = spread(mg_s[...])
    gathered = stack_rows(
        *[sum(tap(a, b) * backs[1 - b] for b in (-1, 0, 1)) for a in (1, 0, -1)]
    )
    pre_grad = (gathered * slope_s[...]).astype(jnp.bfloat16)
    for k in range(nnz):
        gw_in[:, panel(k)] = (tn(tok[:, feats(k)], pre_grad) * loss_scale).astype(jnp.bfloat16)
        dx[:, feats(k)] += nt(pre_grad, w_in[:, panel(k)])

    @pl.when(c == cols - 1)
    def _():
        dx_out[...] = dx[...].astype(jnp.bfloat16)
        kern_out[...] = kern[...].astype(jnp.bfloat16)


def scatter_kernel(
    depth, dx, gw_in, gw_out, kern, dx_mine, in_mine, out_mine, kern_all,
    dx_own, gw_own, dx_near, dx_half, dx_far, dx_sum, dx_last, gw_part, gw_sum, kern_part,
    dx_send, dx_recv, gw_send, gw_recv, kern_send, kern_recv, dx_load, gw_load,
):
    y, r, z, same_chip, across, diagonal = neighbours()
    group = [same_chip, across, diagonal]
    order = (across, diagonal, same_chip, r)
    tokens, features = dx_mine.shape
    rows = in_mine.shape[0]
    lanes = gw_in.shape[1]
    weights = ((gw_in, in_mine), (gw_out, out_mine))
    enter(
        [{"rows": row} for row in group]
        + [{"crop": 1 - y, "rows": row} for row in group]
        + [{"crop": 1 - y}]
        + [{"hid": (z + step) % depth} for step in range(1, depth)]
    )
    started = []

    def go(*args):
        copy = remote(*args)
        copy.start()
        started.append(copy)

    for slot, row in enumerate((diagonal, same_chip)):
        go(dx.at[span(row, tokens), :], dx_near.at[slot], dx_send.at[slot], dx_recv.at[slot], {"rows": same_chip})
    for slot, row in enumerate(order):
        for a in range(2):
            go(
                weights[a][0].at[span((1 - y) * 4 + row, rows), :],
                gw_part.at[a, slot],
                gw_send.at[a, slot],
                gw_recv.at[a, slot],
                {"crop": 1 - y},
            )
    dx_loads = [
        pltpu.make_async_copy(dx.at[span(row, tokens), :], dx_own.at[slot], dx_load.at[slot])
        for slot, row in enumerate((across, r))
    ]
    gw_loads = [
        [
            pltpu.make_async_copy(
                weights[a][0].at[span(y * 4 + row, rows), :], gw_own.at[a, slot], gw_load.at[a, slot]
            )
            for a in range(2)
        ]
        for slot, row in enumerate(order)
    ]
    for load in dx_loads + [load for pair in gw_loads for load in pair]:
        load.start()
    for slot, row in enumerate(group):
        go(kern, kern_part.at[y, r], kern_send.at[slot], kern_recv.at[y, r], {"rows": row})
        go(
            kern,
            kern_part.at[y, r],
            kern_send.at[slot + 3],
            kern_recv.at[y, r],
            {"crop": 1 - y, "rows": row},
        )
    go(kern, kern_part.at[y, r], kern_send.at[6], kern_recv.at[y, r], {"crop": 1 - y})

    def arrived(ref, send_sem, recv_sem, target):
        remote(ref, ref, send_sem, recv_sem, target).wait_recv()

    arrived(dx_near.at[0], dx_send.at[0], dx_recv.at[0], {"rows": same_chip})
    dx_loads[0].wait()
    dx_half[...] = (
        dx_own[0].astype(jnp.float32) + dx_near[0].astype(jnp.float32)
    ).astype(jnp.bfloat16)
    go(dx_half, dx_far, dx_send.at[2], dx_recv.at[2], {"rows": across})
    arrived(dx_near.at[1], dx_send.at[1], dx_recv.at[1], {"rows": same_chip})
    arrived(dx_far, dx_send.at[2], dx_recv.at[2], {"rows": across})
    dx_loads[1].wait()
    for col in range(depth):
        part = slice(col * features, (col + 1) * features)
        dx_sum[col] = (
            dx_own[1, :, part].astype(jnp.float32)
            + dx_near[1, :, part].astype(jnp.float32)
            + dx_far[:, part].astype(jnp.float32)
        ).astype(jnp.bfloat16)
    for step in range(1, depth):
        go(
            dx_sum.at[(z + step) % depth],
            dx_last.at[step - 1],
            dx_send.at[2 + step],
            dx_recv.at[2 + step],
            {"hid": (z + step) % depth},
        )
    for slot, row in enumerate(order):
        for a in range(2):
            arrived(gw_part.at[a, slot], gw_send.at[a, slot], gw_recv.at[a, slot], {"crop": 1 - y})
            gw_loads[slot][a].wait()
            total = (
                gw_own[a, slot].astype(jnp.float32)
                + gw_part[a, slot].astype(jnp.float32)
            ).astype(jnp.bfloat16)
            if slot == 3:
                weights[a][1][:, span(r, lanes)] = total
            else:
                gw_sum[a, slot] = total
                go(
                    gw_sum.at[a, slot],
                    weights[a][1].at[:, span(r, lanes)],
                    gw_send.at[a, 4 + slot],
                    gw_recv.at[a, 4 + slot],
                    {"rows": row},
                )
    total = dx_sum[z].astype(jnp.float32)
    for step in range(1, depth):
        arrived(dx_last.at[step - 1], dx_send.at[2 + step], dx_recv.at[2 + step], {"hid": (z + step) % depth})
        total += dx_last[step - 1].astype(jnp.float32)
    dx_mine[...] = total.astype(jnp.bfloat16)
    kern_part[y, r] = kern[...]
    for row in group:
        for crop in (y, 1 - y):
            arrived(kern_part.at[crop, row], kern_send.at[0], kern_recv.at[crop, row], {"rows": same_chip})
    arrived(kern_part.at[1 - y, r], kern_send.at[0], kern_recv.at[1 - y, r], {"rows": same_chip})
    wide = kern.shape[1]
    for row in range(4):
        kern_all[:, row * wide : (row + 1) * wide] = kern_part[0, row].astype(
            jnp.float32
        ) + kern_part[1, row].astype(jnp.float32)
    for slot, row in enumerate(order[:3]):
        for a in range(2):
            arrived(
                weights[a][1].at[:, span(row, lanes)],
                gw_send.at[a, 4 + slot],
                gw_recv.at[a, 4 + slot],
                {"rows": row},
            )
    for copy in started:
        copy.wait_send()


def finish_kernel(
    all_cols, nnz, in_mine, out_mine, dx_mine, kern_all, in_grad, out_grad, dx_grad, kern_grad
):
    block = in_grad.shape[2]
    dx_grad[...] = dx_mine[...]
    kern_grad[...] = kern_all[: kern_grad.shape[0]]
    for src, dst in ((in_mine, in_grad), (out_mine, out_grad)):
        for c in range(all_cols):
            for k in range(nnz):
                at = (c * nnz + k) * block
                dst[:, k * all_cols + c, :] = src[:, at : at + block].astype(jnp.float32)


def split_hidden(tokens, cotangent, weight_in, weight_out, mix_kernel, block_rows):
    n_rows, depth = lax.axis_size("rows"), lax.axis_size("hid")
    _, height, width, features = tokens.shape
    rows, all_cols, nnz, block = weight_in.shape
    count = height * width
    whole = count * n_rows
    model = features * depth
    cols = all_cols // n_rows
    lanes = cols * nnz * block
    hidden = cols * block
    bf16, f32 = jnp.bfloat16, jnp.float32
    dma, sds = pltpu.SemaphoreType.DMA, jax.ShapeDtypeStruct
    params = functools.partial(pltpu.CompilerParams, vmem_limit_bytes=60 * 1024 * 1024)
    tok_all, cot_all, in_all, out_all = pl.pallas_call(
        functools.partial(gather_kernel, depth),
        name="gather_parts",
        out_shape=[sds((whole, model), bf16)] * 2 + [sds((rows * n_rows, lanes), bf16)] * 2,
        in_specs=[ANY] * 4,
        out_specs=[ANY] * 4,
        scratch_shapes=[
            pltpu.VMEM((2, rows, nnz * all_cols, block), bf16),
            pltpu.VMEM((2, rows, all_cols * nnz * block), bf16),
            pltpu.VMEM((block // 128, rows * all_cols, 128), f32),
            dma((2, 2, depth, 4)),
            dma((2, n_rows, depth)),
            dma((2, 5)),
            dma((2, n_rows, 2)),
            dma((2, 2)),
            dma((2,)),
        ],
        compiler_params=params(collective_id=1, has_side_effects=True),
    )(
        tokens.reshape(count, features),
        cotangent.reshape(count, features),
        weight_in.transpose(0, 2, 1, 3).reshape(rows, nnz * all_cols, block),
        weight_out.transpose(0, 2, 1, 3).reshape(rows, nnz * all_cols, block),
    )
    panel_spec = pl.BlockSpec((block, nnz * block), lambda c: (0, c))
    dx, gw_in, gw_out, kern = pl.pallas_call(
        functools.partial(local_kernel, width, block, cols, nnz),
        name="local_math",
        out_shape=[
            sds((whole, model), bf16),
            sds((block, lanes), bf16),
            sds((block, lanes), bf16),
            sds((16, hidden), bf16),
        ],
        grid=(cols,),
        in_specs=[SMEM, VMEM, VMEM, panel_spec, panel_spec, VMEM],
        out_specs=[VMEM, panel_spec, panel_spec, VMEM],
        scratch_shapes=[pltpu.VMEM((16, hidden), f32), pltpu.VMEM((whole, model), f32)]
        + [pltpu.VMEM((whole, block), f32)] * 4,
        compiler_params=params(),
    )(block_rows.T, tok_all, cot_all, in_all, out_all, mix_kernel)
    out_rows = block // (n_rows * lax.axis_size("crop"))
    dx_mine, in_mine, out_mine, kern_all = pl.pallas_call(
        functools.partial(scatter_kernel, depth),
        name="scatter_sums",
        out_shape=[
            sds((count, features), bf16),
            sds((out_rows, all_cols * nnz * block), bf16),
            sds((out_rows, all_cols * nnz * block), bf16),
            sds((16, hidden * n_rows), f32),
        ],
        in_specs=[ANY] * 3 + [VMEM],
        out_specs=[VMEM] * 4,
        scratch_shapes=[
            pltpu.VMEM((2, count, model), bf16),
            pltpu.VMEM((2, 4, out_rows, lanes), bf16),
            pltpu.VMEM((2, count, model), bf16),
            pltpu.VMEM((count, model), bf16),
            pltpu.VMEM((count, model), bf16),
            pltpu.VMEM((depth, count, features), bf16),
            pltpu.VMEM((depth - 1, count, features), bf16),
            pltpu.VMEM((2, 4, out_rows, lanes), bf16),
            pltpu.VMEM((2, 3, out_rows, lanes), bf16),
            pltpu.VMEM((2, n_rows, 16, hidden), bf16),
            dma((2 + depth,)),
            dma((2 + depth,)),
            dma((2, 7)),
            dma((2, 7)),
            dma((7,)),
            dma((2, n_rows)),
            dma((2,)),
            dma((2, 4)),
        ],
        compiler_params=params(collective_id=2, has_side_effects=True),
    )(dx, gw_in, gw_out, kern)
    step = 8
    part = pl.BlockSpec((count * step // out_rows, features), lambda i: (i, 0))
    flat_spec = pl.BlockSpec((step, all_cols * nnz * block), lambda i: (i, 0))
    grad_spec = pl.BlockSpec((step, nnz * all_cols, block), lambda i: (i, 0, 0))
    in_grad, out_grad, dx_grad, kern_grad = pl.pallas_call(
        functools.partial(finish_kernel, all_cols, nnz),
        name="finish_weights",
        grid=(out_rows // step,),
        out_shape=[sds((out_rows, nnz * all_cols, block), f32)] * 2
        + [sds((count, features), bf16), sds(mix_kernel.shape, f32)],
        in_specs=[flat_spec] * 2 + [part, VMEM],
        out_specs=[grad_spec] * 2 + [part, VMEM],
        compiler_params=params(),
    )(in_mine, out_mine, dx_mine, kern_all)
    in_grad, out_grad = [
        grad.reshape(out_rows, nnz, all_cols, block).transpose(0, 2, 1, 3) for grad in (in_grad, out_grad)
    ]
    return (dx_grad.reshape(tokens.shape), in_grad, out_grad, kern_grad)


def padded(shard, sides, width):
    for axis, dim in sides:
        devices, length = (lax.axis_size(axis), shard.shape[dim])
        up = [(i, (i + 1) % devices) for i in range(devices - 1)]
        down = [(j, i) for i, j in up]
        last = lax.slice_in_dim(shard, length - width, length, axis=dim)
        initial = lax.slice_in_dim(shard, 0, width, axis=dim)
        before = lax.ppermute(last, axis, up)
        after = lax.ppermute(initial, axis, down)
        shard = jnp.concatenate([before, shard, after], axis=dim)
    return shard


def gelu_pair(preact):
    inner = root_two_pi * (preact + cubic_coef * preact * preact * preact)
    tanh_val = jnp.tanh(inner)
    gelu_out = 0.5 * preact * (1.0 + tanh_val)
    slopes = 0.5 * (1.0 + tanh_val) + 0.5 * preact * (1.0 - tanh_val * tanh_val) * root_two_pi * (
        1.0 + 3.0 * cubic_coef * preact * preact
    )
    return (gelu_out, slopes)


def on_device(tokens, cotangent, weight_in, weight_out, mix_kernel, block_rows):
    in_panel, out_panel = (
        lax.all_gather(weight_in, "rows", axis=0, tiled=True),
        lax.all_gather(weight_out, "rows", axis=0, tiled=True),
    )
    tok_full, cot_full = (
        lax.all_gather(tokens, "hid", axis=3, tiled=True),
        lax.all_gather(cotangent, "hid", axis=3, tiled=True),
    )
    crop_count, height, grid_width, depth_all = tok_full.shape
    tok_count = crop_count * height * grid_width
    block_size = in_panel.shape[0]
    col_count = in_panel.shape[1]
    nnz_count = in_panel.shape[2]
    block_count = depth_all // block_size
    hidden_local = col_count * block_size
    flat_rows = block_rows.reshape(-1)
    in_select = jnp.take(
        tok_full.reshape(tok_count, block_count, block_size), flat_rows, axis=1
    ).reshape(tok_count, col_count, nnz_count, block_size)
    grad_select = jnp.take(
        cot_full.reshape(tok_count, block_count, block_size), flat_rows, axis=1
    ).reshape(tok_count, col_count, nnz_count, block_size)
    pre_act = jnp.einsum("tckb,bcke->tce", in_select, in_panel, preferred_element_type=jnp.float32)
    gelu_out, slopes = gelu_pair(pre_act)
    active = gelu_out.astype(jnp.bfloat16).reshape(crop_count, height, grid_width, hidden_local)
    act_rim = padded(active, (("rows", 1),), 1)
    mix_grad = (
        jnp.einsum("tckd,fckd->tcf", grad_select, out_panel, preferred_element_type=jnp.float32)
        .astype(jnp.bfloat16)
        .reshape(crop_count, height, grid_width, hidden_local)
    )
    grad_rim = padded(mix_grad, (("rows", 1),), 1)
    act_pad = jnp.pad(act_rim.astype(jnp.float32), ((0, 0), (0, 0), (1, 1), (0, 0)))
    grad_pad = jnp.pad(grad_rim.astype(jnp.float32), ((0, 0), (0, 0), (1, 1), (0, 0)))
    grad_grid = mix_grad.astype(jnp.float32)
    mix_sum = jnp.zeros((crop_count, height, grid_width, hidden_local), jnp.float32)
    act_grad = jnp.zeros((crop_count, height, grid_width, hidden_local), jnp.float32)
    kern_terms = []
    for row_off in range(3):
        for col_off in range(3):
            tap = mix_kernel[3 * row_off + col_off]
            shifted = act_pad[:, row_off : row_off + height, col_off : col_off + grid_width]
            mix_sum = mix_sum + tap * shifted
            act_grad = (
                act_grad
                + tap
                * grad_pad[
                    :, 2 - row_off : 2 - row_off + height, 2 - col_off : 2 - col_off + grid_width
                ]
            )
            kern_terms.append(jnp.sum(shifted * grad_grid, axis=(0, 1, 2)))
    kern_local = jnp.stack(kern_terms, axis=0) * loss_scale
    mix_out = mix_sum.astype(jnp.bfloat16).reshape(tok_count, col_count, block_size)
    pre_grad = (act_grad.reshape(tok_count, col_count, block_size) * slopes).astype(jnp.bfloat16)
    kern_total = lax.psum(kern_local.astype(jnp.bfloat16), ("crop", "rows")).astype(jnp.float32)
    back_select = jnp.einsum(
        "tce,bcke->tckb", pre_grad, in_panel, preferred_element_type=jnp.float32
    )
    one_hot = (
        block_rows[:, :, None] == jnp.arange(block_count, dtype=jnp.int32)[None, None, :]
    ).astype(jnp.float32)
    token_terms = jnp.einsum(
        "tckb,ckr->trb", back_select, one_hot, precision=lax.Precision.HIGHEST
    ).reshape(crop_count, height, grid_width, depth_all)
    grad_tokens = lax.psum_scatter(
        token_terms.astype(jnp.bfloat16), "hid", scatter_dimension=3, tiled=True
    )
    first_term = jnp.einsum(
        "tckb,tce->bcke", in_select, pre_grad, preferred_element_type=jnp.float32
    )
    second_term = jnp.einsum(
        "tcf,tckd->fckd", mix_out, grad_select, preferred_element_type=jnp.float32
    )
    share_sums = lax.psum_scatter(
        (jnp.stack([first_term, second_term], axis=1) * loss_scale).astype(jnp.bfloat16),
        ("crop", "rows"),
        scatter_dimension=0,
        tiled=True,
    ).astype(jnp.float32)
    return (grad_tokens, share_sums[:, 0], share_sums[:, 1], kern_total)


def solution(mesh):
    placed = (
        P("crop", "rows", None, "hid"),
        P("crop", "rows", None, "hid"),
        P("rows", "hid", None, None),
        P("rows", "hid", None, None),
        P(None, "hid"),
        P("hid", None),
    )
    n_crop, n_rows = mesh.shape["crop"], mesh.shape["rows"]
    n_hid = mesh.shape["hid"]

    def step(tokens, cotangent, weight_in, weight_out, mix_kernel, block_rows):
        fits = (
            n_crop == 2
            and n_rows == 4
            and tokens.shape[0] == 1
            and weight_in.shape[1] % n_rows == 0
            and tokens.shape[1] * tokens.shape[2] * n_rows * tokens.shape[3] * n_hid <= 2**22
        )
        chosen = split_hidden if fits else on_device
        return chosen(tokens, cotangent, weight_in, weight_out, mix_kernel, block_rows)

    return jax.shard_map(
        step,
        mesh=mesh,
        in_specs=placed,
        out_specs=(
            P("crop", "rows", None, "hid"),
            P(("crop", "rows"), "hid", None, None),
            P(("crop", "rows"), "hid", None, None),
            P(None, "hid"),
        ),
        check_vma=False,
    )
```

```python
import functools

import jax
import jax.numpy as jnp
from jax import lax
from jax.experimental import pallas as pl
from jax.experimental.pallas import tpu as pltpu
from jax.sharding import PartitionSpec as P

root_two_pi = 0.7978845608
cubic_coef = 0.044715
loss_scale = 0.03125

MESH_ID = pl.DeviceIdType.MESH
ANY = pl.BlockSpec(memory_space=pl.ANY)
VMEM = pl.BlockSpec(memory_space=pltpu.VMEM)
SMEM = pl.BlockSpec(memory_space=pltpu.SMEM)


def span(start, size):
    return pl.ds(pl.multiple_of(start * size, size), size)


def neighbours():
    y, r, z = lax.axis_index("crop"), lax.axis_index("rows"), lax.axis_index("hid")
    x, core = r // 2, r % 2
    same_chip = x * 2 + (1 - core)
    across = (1 - x) * 2 + core
    diagonal = (1 - x) * 2 + (1 - core)
    return y, r, z, same_chip, across, diagonal


def enter(partners):
    barrier = pltpu.get_barrier_semaphore()
    for partner in partners:
        pl.semaphore_signal(barrier, inc=1, device_id=partner, device_id_type=MESH_ID)
    pl.semaphore_wait(barrier, len(partners))


def remote(src, dst, send_sem, recv_sem, target):
    return pltpu.make_async_remote_copy(
        src_ref=src,
        dst_ref=dst,
        send_sem=send_sem,
        recv_sem=recv_sem,
        device_id=target,
        device_id_type=MESH_ID,
    )


def gather_kernel(
    depth, tok, cot, w_in, w_out, tok_all, cot_all, in_all, out_all,
    raw, flat, stage, tok_send, tok_recv, w_send, w_recv, own_sem, raw_sem,
):
    y, r, z, same_chip, across, diagonal = neighbours()
    tokens, features = tok.shape
    rows = w_in.shape[0]
    lanes = in_all.shape[1]
    half = rows // 2
    block = w_in.shape[2]
    all_cols = stage.shape[1] // rows
    nnz = w_in.shape[1] // all_cols
    loads = [
        pltpu.make_async_copy(src, raw.at[a], raw_sem.at[a]) for a, src in enumerate((w_in, w_out))
    ]
    for load in loads:
        load.start()
    enter(
        [{"rows": same_chip}, {"rows": across}, {"rows": diagonal}, {"crop": 1 - y}]
        + [{"hid": (z + step) % depth} for step in range(1, depth)]
    )
    streams = ((tok, tok_all), (cot, cot_all))
    panels = ((flat.at[0], in_all), (flat.at[1], out_all))
    targets = ({"hid": z + 1}, {"hid": z - 1}, {"rows": across}, {"rows": same_chip})
    has_up, has_down = z + 1 < depth, z >= 1
    sends, local = [], []

    def launch(make, have=None):
        sends.append((make, have))
        if have is None:
            make().start()
        else:
            pl.when(have)(lambda: make().start())

    def piece(full, row, col):
        return full.at[span(row, tokens), span(col, features)]

    def pass_on(a, which, col, kind, have=None, own=False):
        def make():
            row = (r, across)[which]
            part = piece(streams[a][1], row, col)
            return remote(
                streams[a][0] if own else part,
                part,
                tok_send.at[a, which, col, kind],
                tok_recv.at[a, row, col],
                targets[kind],
            )

        launch(make, have)

    def await_piece(a, row, col, have=None):
        def wait():
            part = piece(streams[a][1], row, col)
            remote(
                part, part, tok_send.at[a, 0, 0, 3], tok_recv.at[a, row, col], {"rows": same_chip}
            ).wait_recv()

        if have is None:
            wait()
        else:
            pl.when(have)(wait)

    def half_rows(full, row, h):
        return full.at[pl.ds(pl.multiple_of(row * rows + h * half, half), half), :]

    def flatten(a):
        def turn(k, carry):
            for h in range(block // 128):
                part = raw[a, :, span(k, all_cols), h * 128 : (h + 1) * 128]
                stage[h] = part.astype(jnp.float32).reshape(rows * all_cols, 128)
            for c in range(all_cols):
                for h in range(block // 128):
                    flat[a, :, pl.ds(pl.multiple_of((c * nnz + k) * block + h * 128, 128), 128)] = stage[
                        h, pl.ds(c, rows, stride=all_cols), :
                    ].astype(jnp.bfloat16)
            return carry

        lax.fori_loop(0, nnz, turn, 0)

    def give_weights(a):
        src, full = panels[a]
        loads[a].wait()
        flatten(a)
        for slot, dest in ((1, across), (2, diagonal)):
            launch(
                lambda slot=slot, dest=dest: remote(
                    src.at[span(y, half), span(dest, lanes)],
                    half_rows(full, r, y),
                    w_send.at[a, slot],
                    w_recv.at[a, r, y],
                    {"rows": dest},
                )
            )
        launch(
            lambda: remote(
                src.at[:, span(same_chip, lanes)],
                full.at[span(r, rows), :],
                w_send.at[a, 0],
                w_recv.at[a, r, 0],
                {"rows": same_chip},
            )
        )
        keep = pltpu.make_async_copy(
            src.at[:, span(r, lanes)], full.at[span(r, rows), :], own_sem.at[a, 1]
        )
        keep.start()
        local.append(keep)

    def mirror_weights(a):
        full = panels[a][1]
        for slot, row in ((3, across), (4, diagonal)):
            part = half_rows(full, row, y)
            remote(part, part, w_send.at[a, slot], w_recv.at[a, row, y], {"rows": row}).wait_recv()
            launch(
                lambda slot=slot, row=row, part=part: remote(
                    part, part, w_send.at[a, slot], w_recv.at[a, row, y], {"crop": 1 - y}
                )
            )

    def line_step(step):
        for below in (True, False):
            col = z - step if below else z + step
            have = col >= 0 if below else col < depth
            onward = jnp.logical_and(have, has_up if below else has_down)
            for a, which in ((0, 0), (1, 0), (1, 1)):
                await_piece(a, (r, across)[which], col, have)
                pass_on(a, which, col, 0 if below else 1, onward)
                if a == 0:
                    pass_on(a, which, col, 2, have)
                pass_on(a, which, col, 3, have)

    for a, kind in ((1, 2), (0, 0), (0, 1), (1, 0), (1, 1), (0, 2), (0, 3), (1, 3)):
        pass_on(a, 0, z, kind, (has_up, has_down, None, None)[kind], own=True)
    for a in range(2):
        keep = pltpu.make_async_copy(streams[a][0], piece(streams[a][1], r, z), own_sem.at[a, 0])
        keep.start()
        local.append(keep)
    give_weights(0)
    await_piece(1, across, z)
    for kind in (0, 1, 3):
        pass_on(1, 1, z, kind, (has_up, has_down, None, None)[kind])
    give_weights(1)
    for step in range(1, depth):
        line_step(step)
        if step <= 2:
            mirror_weights(step - 1)
    for a in range(depth - 1, 2):
        mirror_weights(a)
    for step in range(depth):
        col = (z + step) % depth
        await_piece(0, across, col)
        pass_on(0, 1, col, 3)
    for a in range(2):
        full = panels[a][1]
        part = full.at[span(same_chip, rows), :]
        remote(
            part, part, w_send.at[a, 0], w_recv.at[a, same_chip, 0], {"rows": same_chip}
        ).wait_recv()
        for row in (across, diagonal):
            part = half_rows(full, row, 1 - y)
            remote(
                part, part, w_send.at[a, 0], w_recv.at[a, row, 1 - y], {"crop": 1 - y}
            ).wait_recv()
        for row in (same_chip, diagonal):
            for step in range(depth):
                await_piece(a, row, (z + step) % depth)
    for copy in local:
        copy.wait()
    for make, have in sends:
        if have is None:
            make().wait_send()
        else:
            pl.when(have)(lambda make=make: make().wait_send())


def nt(a, b):
    return lax.dot_general(a, b, (((1,), (1,)), ((), ())), preferred_element_type=jnp.float32)


def tn(a, b):
    return lax.dot_general(a, b, (((0,), (0,)), ((), ())), preferred_element_type=jnp.float32)


def local_kernel(
    width, block, cols, nnz, ids, tok, cot, w_in, w_out, taps,
    dx_out, gw_in, gw_out, kern_out, kern, dx, pre_s, act_s, slope_s, mg_s,
):
    count = tok.shape[0]
    me = lax.axis_index("rows")
    c = pl.program_id(0)
    place = lax.broadcasted_iota(jnp.int32, (count, block), 0) % width

    @pl.when(c == 0)
    def _():
        dx[...] = jnp.zeros_like(dx)
        kern[...] = jnp.zeros_like(kern)

    def spread(value):
        before = jnp.where(place == 0, 0.0, pltpu.roll(value, 1, 0))
        after = jnp.where(place == width - 1, 0.0, pltpu.roll(value, count - 1, 0))
        return (before, value, after)

    def stack_rows(up, mid, down):
        edge = jnp.zeros((width, block), jnp.float32)
        return (
            mid
            + jnp.concatenate([edge, up[:-width]], axis=0)
            + jnp.concatenate([down[width:], edge], axis=0)
        )

    hidden = span(c, block)

    def feats(k):
        return span(ids[k, me * cols + c], block)

    def panel(k):
        return slice(k * block, (k + 1) * block)

    pre = jnp.dot(tok[:, feats(0)], w_in[:, panel(0)], preferred_element_type=jnp.float32)
    for k in range(1, nnz):
        pre += jnp.dot(tok[:, feats(k)], w_in[:, panel(k)], preferred_element_type=jnp.float32)
    pre_s[...] = pre
    mg = nt(cot[:, feats(0)], w_out[:, panel(0)])
    for k in range(1, nnz):
        mg += nt(cot[:, feats(k)], w_out[:, panel(k)])
    mg_s[...] = mg.astype(jnp.bfloat16).astype(jnp.float32)
    p = pre_s[...]
    t = jnp.tanh(root_two_pi * (p + cubic_coef * p * p * p))
    act_s[...] = (0.5 * p * (1.0 + t)).astype(jnp.bfloat16).astype(jnp.float32)
    slope_s[...] = 0.5 * (1.0 + t) + 0.5 * p * (1.0 - t * t) * root_two_pi * (
        1.0 + 3.0 * cubic_coef * p * p
    )

    def tap(a, b):
        row = 3 * (a + 1) + (b + 1)
        return taps[row : row + 1, span(me * cols + c, block)]

    acts = spread(act_s[...])
    mixed = stack_rows(
        *[sum(tap(a, b) * acts[b + 1] for b in (-1, 0, 1)) for a in (-1, 0, 1)]
    ).astype(jnp.bfloat16)
    grads = mg_s[...]
    for b in (-1, 0, 1):
        seen = acts[b + 1]
        sums = (
            jnp.sum(seen[:-width] * grads[width:], axis=0, keepdims=True),
            jnp.sum(seen * grads, axis=0, keepdims=True),
            jnp.sum(seen[width:] * grads[:-width], axis=0, keepdims=True),
        )
        for a in (-1, 0, 1):
            row = 3 * (a + 1) + (b + 1)
            kern[row : row + 1, hidden] = sums[a + 1] * loss_scale
    for k in range(nnz):
        gw_out[:, panel(k)] = (tn(mixed, cot[:, feats(k)]) * loss_scale).astype(jnp.bfloat16)
    backs = spread(mg_s[...])
    gathered = stack_rows(
        *[sum(tap(a, b) * backs[1 - b] for b in (-1, 0, 1)) for a in (1, 0, -1)]
    )
    pre_grad = (gathered * slope_s[...]).astype(jnp.bfloat16)
    for k in range(nnz):
        gw_in[:, panel(k)] = (tn(tok[:, feats(k)], pre_grad) * loss_scale).astype(jnp.bfloat16)
        dx[:, feats(k)] += nt(pre_grad, w_in[:, panel(k)])

    @pl.when(c == cols - 1)
    def _():
        dx_out[...] = dx[...].astype(jnp.bfloat16)
        kern_out[...] = kern[...].astype(jnp.bfloat16)


def scatter_kernel(
    depth, dx, gw_in, gw_out, kern, dx_mine, in_mine, out_mine, kern_all,
    dx_own, gw_own, dx_near, dx_half, dx_far, dx_sum, dx_last, gw_part, gw_sum, kern_part,
    dx_send, dx_recv, gw_send, gw_recv, kern_send, kern_recv, dx_load, gw_load,
):
    y, r, z, same_chip, across, diagonal = neighbours()
    group = [same_chip, across, diagonal]
    order = (across, diagonal, same_chip, r)
    tokens, features = dx_mine.shape
    rows = in_mine.shape[0]
    lanes = gw_in.shape[1]
    weights = ((gw_in, in_mine), (gw_out, out_mine))
    enter(
        [{"rows": row} for row in group]
        + [{"crop": 1 - y, "rows": row} for row in group]
        + [{"crop": 1 - y}]
        + [{"hid": (z + step) % depth} for step in range(1, depth)]
    )
    started = []

    def go(*args):
        copy = remote(*args)
        copy.start()
        started.append(copy)

    for slot, row in enumerate((diagonal, same_chip)):
        go(dx.at[span(row, tokens), :], dx_near.at[slot], dx_send.at[slot], dx_recv.at[slot], {"rows": same_chip})
    for slot, row in enumerate(order):
        for a in range(2):
            go(
                weights[a][0].at[span((1 - y) * 4 + row, rows), :],
                gw_part.at[a, slot],
                gw_send.at[a, slot],
                gw_recv.at[a, slot],
                {"crop": 1 - y},
            )
    dx_loads = [
        pltpu.make_async_copy(dx.at[span(row, tokens), :], dx_own.at[slot], dx_load.at[slot])
        for slot, row in enumerate((across, r))
    ]
    gw_loads = [
        [
            pltpu.make_async_copy(
                weights[a][0].at[span(y * 4 + row, rows), :], gw_own.at[a, slot], gw_load.at[a, slot]
            )
            for a in range(2)
        ]
        for slot, row in enumerate(order)
    ]
    for load in dx_loads + [load for pair in gw_loads for load in pair]:
        load.start()
    for slot, row in enumerate(group):
        go(kern, kern_part.at[y, r], kern_send.at[slot], kern_recv.at[y, r], {"rows": row})
        go(
            kern,
            kern_part.at[y, r],
            kern_send.at[slot + 3],
            kern_recv.at[y, r],
            {"crop": 1 - y, "rows": row},
        )
    go(kern, kern_part.at[y, r], kern_send.at[6], kern_recv.at[y, r], {"crop": 1 - y})

    def arrived(ref, send_sem, recv_sem, target):
        remote(ref, ref, send_sem, recv_sem, target).wait_recv()

    arrived(dx_near.at[0], dx_send.at[0], dx_recv.at[0], {"rows": same_chip})
    dx_loads[0].wait()
    dx_half[...] = (
        dx_own[0].astype(jnp.float32) + dx_near[0].astype(jnp.float32)
    ).astype(jnp.bfloat16)
    go(dx_half, dx_far, dx_send.at[2], dx_recv.at[2], {"rows": across})
    arrived(dx_near.at[1], dx_send.at[1], dx_recv.at[1], {"rows": same_chip})
    arrived(dx_far, dx_send.at[2], dx_recv.at[2], {"rows": across})
    dx_loads[1].wait()
    for col in range(depth):
        part = slice(col * features, (col + 1) * features)
        dx_sum[col] = (
            dx_own[1, :, part].astype(jnp.float32)
            + dx_near[1, :, part].astype(jnp.float32)
            + dx_far[:, part].astype(jnp.float32)
        ).astype(jnp.bfloat16)
    for step in range(1, depth):
        go(
            dx_sum.at[(z + step) % depth],
            dx_last.at[step - 1],
            dx_send.at[2 + step],
            dx_recv.at[2 + step],
            {"hid": (z + step) % depth},
        )
    for slot, row in enumerate(order):
        for a in range(2):
            arrived(gw_part.at[a, slot], gw_send.at[a, slot], gw_recv.at[a, slot], {"crop": 1 - y})
            gw_loads[slot][a].wait()
            total = (
                gw_own[a, slot].astype(jnp.float32)
                + gw_part[a, slot].astype(jnp.float32)
            ).astype(jnp.bfloat16)
            if slot == 3:
                weights[a][1][:, span(r, lanes)] = total
            else:
                gw_sum[a, slot] = total
                go(
                    gw_sum.at[a, slot],
                    weights[a][1].at[:, span(r, lanes)],
                    gw_send.at[a, 4 + slot],
                    gw_recv.at[a, 4 + slot],
                    {"rows": row},
                )
    total = dx_sum[z].astype(jnp.float32)
    for step in range(1, depth):
        arrived(dx_last.at[step - 1], dx_send.at[2 + step], dx_recv.at[2 + step], {"hid": (z + step) % depth})
        total += dx_last[step - 1].astype(jnp.float32)
    dx_mine[...] = total.astype(jnp.bfloat16)
    kern_part[y, r] = kern[...]
    for row in group:
        for crop in (y, 1 - y):
            arrived(kern_part.at[crop, row], kern_send.at[0], kern_recv.at[crop, row], {"rows": same_chip})
    arrived(kern_part.at[1 - y, r], kern_send.at[0], kern_recv.at[1 - y, r], {"rows": same_chip})
    wide = kern.shape[1]
    for row in range(4):
        kern_all[:, row * wide : (row + 1) * wide] = kern_part[0, row].astype(
            jnp.float32
        ) + kern_part[1, row].astype(jnp.float32)
    for slot, row in enumerate(order[:3]):
        for a in range(2):
            arrived(
                weights[a][1].at[:, span(row, lanes)],
                gw_send.at[a, 4 + slot],
                gw_recv.at[a, 4 + slot],
                {"rows": row},
            )
    for copy in started:
        copy.wait_send()


def finish_kernel(
    all_cols, nnz, in_mine, out_mine, dx_mine, kern_all, in_grad, out_grad, dx_grad, kern_grad
):
    block = in_grad.shape[2]
    dx_grad[...] = dx_mine[...]
    kern_grad[...] = kern_all[: kern_grad.shape[0]]
    for src, dst in ((in_mine, in_grad), (out_mine, out_grad)):
        for c in range(all_cols):
            for k in range(nnz):
                at = (c * nnz + k) * block
                dst[:, k * all_cols + c, :] = src[:, at : at + block].astype(jnp.float32)


def split_hidden(tokens, cotangent, weight_in, weight_out, mix_kernel, block_rows):
    n_rows, depth = lax.axis_size("rows"), lax.axis_size("hid")
    _, height, width, features = tokens.shape
    rows, all_cols, nnz, block = weight_in.shape
    count = height * width
    whole = count * n_rows
    model = features * depth
    cols = all_cols // n_rows
    lanes = cols * nnz * block
    hidden = cols * block
    bf16, f32 = jnp.bfloat16, jnp.float32
    dma, sds = pltpu.SemaphoreType.DMA, jax.ShapeDtypeStruct
    params = functools.partial(pltpu.CompilerParams, vmem_limit_bytes=60 * 1024 * 1024)
    tok_all, cot_all, in_all, out_all = pl.pallas_call(
        functools.partial(gather_kernel, depth),
        name="gather_parts",
        out_shape=[sds((whole, model), bf16)] * 2 + [sds((rows * n_rows, lanes), bf16)] * 2,
        in_specs=[ANY] * 4,
        out_specs=[ANY] * 4,
        scratch_shapes=[
            pltpu.VMEM((2, rows, nnz * all_cols, block), bf16),
            pltpu.VMEM((2, rows, all_cols * nnz * block), bf16),
            pltpu.VMEM((block // 128, rows * all_cols, 128), f32),
            dma((2, 2, depth, 4)),
            dma((2, n_rows, depth)),
            dma((2, 5)),
            dma((2, n_rows, 2)),
            dma((2, 2)),
            dma((2,)),
        ],
        compiler_params=params(collective_id=1, has_side_effects=True),
    )(
        tokens.reshape(count, features),
        cotangent.reshape(count, features),
        weight_in.transpose(0, 2, 1, 3).reshape(rows, nnz * all_cols, block),
        weight_out.transpose(0, 2, 1, 3).reshape(rows, nnz * all_cols, block),
    )
    panel_spec = pl.BlockSpec((block, nnz * block), lambda c: (0, c))
    dx, gw_in, gw_out, kern = pl.pallas_call(
        functools.partial(local_kernel, width, block, cols, nnz),
        name="local_math",
        out_shape=[
            sds((whole, model), bf16),
            sds((block, lanes), bf16),
            sds((block, lanes), bf16),
            sds((16, hidden), bf16),
        ],
        grid=(cols,),
        in_specs=[SMEM, VMEM, VMEM, panel_spec, panel_spec, VMEM],
        out_specs=[VMEM, panel_spec, panel_spec, VMEM],
        scratch_shapes=[pltpu.VMEM((16, hidden), f32), pltpu.VMEM((whole, model), f32)]
        + [pltpu.VMEM((whole, block), f32)] * 4,
        compiler_params=params(),
    )(block_rows.T, tok_all, cot_all, in_all, out_all, mix_kernel)
    out_rows = block // (n_rows * lax.axis_size("crop"))
    dx_mine, in_mine, out_mine, kern_all = pl.pallas_call(
        functools.partial(scatter_kernel, depth),
        name="scatter_sums",
        out_shape=[
            sds((count, features), bf16),
            sds((out_rows, all_cols * nnz * block), bf16),
            sds((out_rows, all_cols * nnz * block), bf16),
            sds((16, hidden * n_rows), f32),
        ],
        in_specs=[ANY] * 3 + [VMEM],
        out_specs=[VMEM] * 4,
        scratch_shapes=[
            pltpu.VMEM((2, count, model), bf16),
            pltpu.VMEM((2, 4, out_rows, lanes), bf16),
            pltpu.VMEM((2, count, model), bf16),
            pltpu.VMEM((count, model), bf16),
            pltpu.VMEM((count, model), bf16),
            pltpu.VMEM((depth, count, features), bf16),
            pltpu.VMEM((depth - 1, count, features), bf16),
            pltpu.VMEM((2, 4, out_rows, lanes), bf16),
            pltpu.VMEM((2, 3, out_rows, lanes), bf16),
            pltpu.VMEM((2, n_rows, 16, hidden), bf16),
            dma((2 + depth,)),
            dma((2 + depth,)),
            dma((2, 7)),
            dma((2, 7)),
            dma((7,)),
            dma((2, n_rows)),
            dma((2,)),
            dma((2, 4)),
        ],
        compiler_params=params(collective_id=2, has_side_effects=True),
    )(dx, gw_in, gw_out, kern)
    step = 8
    part = pl.BlockSpec((count * step // out_rows, features), lambda i: (i, 0))
    flat_spec = pl.BlockSpec((step, all_cols * nnz * block), lambda i: (i, 0))
    grad_spec = pl.BlockSpec((step, nnz * all_cols, block), lambda i: (i, 0, 0))
    in_grad, out_grad, dx_grad, kern_grad = pl.pallas_call(
        functools.partial(finish_kernel, all_cols, nnz),
        name="finish_weights",
        grid=(out_rows // step,),
        out_shape=[sds((out_rows, nnz * all_cols, block), f32)] * 2
        + [sds((count, features), bf16), sds(mix_kernel.shape, f32)],
        in_specs=[flat_spec] * 2 + [part, VMEM],
        out_specs=[grad_spec] * 2 + [part, VMEM],
        compiler_params=params(),
    )(in_mine, out_mine, dx_mine, kern_all)
    in_grad, out_grad = [
        grad.reshape(out_rows, nnz, all_cols, block).transpose(0, 2, 1, 3) for grad in (in_grad, out_grad)
    ]
    return (dx_grad.reshape(tokens.shape), in_grad, out_grad, kern_grad)


def padded(shard, sides, width):
    for axis, dim in sides:
        devices, length = (lax.axis_size(axis), shard.shape[dim])
        up = [(i, (i + 1) % devices) for i in range(devices - 1)]
        down = [(j, i) for i, j in up]
        last = lax.slice_in_dim(shard, length - width, length, axis=dim)
        initial = lax.slice_in_dim(shard, 0, width, axis=dim)
        before = lax.ppermute(last, axis, up)
        after = lax.ppermute(initial, axis, down)
        shard = jnp.concatenate([before, shard, after], axis=dim)
    return shard


def gelu_pair(preact):
    inner = root_two_pi * (preact + cubic_coef * preact * preact * preact)
    tanh_val = jnp.tanh(inner)
    gelu_out = 0.5 * preact * (1.0 + tanh_val)
    slopes = 0.5 * (1.0 + tanh_val) + 0.5 * preact * (1.0 - tanh_val * tanh_val) * root_two_pi * (
        1.0 + 3.0 * cubic_coef * preact * preact
    )
    return (gelu_out, slopes)


def on_device(tokens, cotangent, weight_in, weight_out, mix_kernel, block_rows):
    in_panel, out_panel = (
        lax.all_gather(weight_in, "rows", axis=0, tiled=True),
        lax.all_gather(weight_out, "rows", axis=0, tiled=True),
    )
    tok_full, cot_full = (
        lax.all_gather(tokens, "hid", axis=3, tiled=True),
        lax.all_gather(cotangent, "hid", axis=3, tiled=True),
    )
    crop_count, height, grid_width, depth_all = tok_full.shape
    tok_count = crop_count * height * grid_width
    block_size = in_panel.shape[0]
    col_count = in_panel.shape[1]
    nnz_count = in_panel.shape[2]
    block_count = depth_all // block_size
    hidden_local = col_count * block_size
    flat_rows = block_rows.reshape(-1)
    in_select = jnp.take(
        tok_full.reshape(tok_count, block_count, block_size), flat_rows, axis=1
    ).reshape(tok_count, col_count, nnz_count, block_size)
    grad_select = jnp.take(
        cot_full.reshape(tok_count, block_count, block_size), flat_rows, axis=1
    ).reshape(tok_count, col_count, nnz_count, block_size)
    pre_act = jnp.einsum("tckb,bcke->tce", in_select, in_panel, preferred_element_type=jnp.float32)
    gelu_out, slopes = gelu_pair(pre_act)
    active = gelu_out.astype(jnp.bfloat16).reshape(crop_count, height, grid_width, hidden_local)
    act_rim = padded(active, (("rows", 1),), 1)
    mix_grad = (
        jnp.einsum("tckd,fckd->tcf", grad_select, out_panel, preferred_element_type=jnp.float32)
        .astype(jnp.bfloat16)
        .reshape(crop_count, height, grid_width, hidden_local)
    )
    grad_rim = padded(mix_grad, (("rows", 1),), 1)
    act_pad = jnp.pad(act_rim.astype(jnp.float32), ((0, 0), (0, 0), (1, 1), (0, 0)))
    grad_pad = jnp.pad(grad_rim.astype(jnp.float32), ((0, 0), (0, 0), (1, 1), (0, 0)))
    grad_grid = mix_grad.astype(jnp.float32)
    mix_sum = jnp.zeros((crop_count, height, grid_width, hidden_local), jnp.float32)
    act_grad = jnp.zeros((crop_count, height, grid_width, hidden_local), jnp.float32)
    kern_terms = []
    for row_off in range(3):
        for col_off in range(3):
            tap = mix_kernel[3 * row_off + col_off]
            shifted = act_pad[:, row_off : row_off + height, col_off : col_off + grid_width]
            mix_sum = mix_sum + tap * shifted
            act_grad = (
                act_grad
                + tap
                * grad_pad[
                    :, 2 - row_off : 2 - row_off + height, 2 - col_off : 2 - col_off + grid_width
                ]
            )
            kern_terms.append(jnp.sum(shifted * grad_grid, axis=(0, 1, 2)))
    kern_local = jnp.stack(kern_terms, axis=0) * loss_scale
    mix_out = mix_sum.astype(jnp.bfloat16).reshape(tok_count, col_count, block_size)
    pre_grad = (act_grad.reshape(tok_count, col_count, block_size) * slopes).astype(jnp.bfloat16)
    kern_total = lax.psum(kern_local.astype(jnp.bfloat16), ("crop", "rows")).astype(jnp.float32)
    back_select = jnp.einsum(
        "tce,bcke->tckb", pre_grad, in_panel, preferred_element_type=jnp.float32
    )
    one_hot = (
        block_rows[:, :, None] == jnp.arange(block_count, dtype=jnp.int32)[None, None, :]
    ).astype(jnp.float32)
    token_terms = jnp.einsum(
        "tckb,ckr->trb", back_select, one_hot, precision=lax.Precision.HIGHEST
    ).reshape(crop_count, height, grid_width, depth_all)
    grad_tokens = lax.psum_scatter(
        token_terms.astype(jnp.bfloat16), "hid", scatter_dimension=3, tiled=True
    )
    first_term = jnp.einsum(
        "tckb,tce->bcke", in_select, pre_grad, preferred_element_type=jnp.float32
    )
    second_term = jnp.einsum(
        "tcf,tckd->fckd", mix_out, grad_select, preferred_element_type=jnp.float32
    )
    share_sums = lax.psum_scatter(
        (jnp.stack([first_term, second_term], axis=1) * loss_scale).astype(jnp.bfloat16),
        ("crop", "rows"),
        scatter_dimension=0,
        tiled=True,
    ).astype(jnp.float32)
    return (grad_tokens, share_sums[:, 0], share_sums[:, 1], kern_total)


def solution(mesh):
    placed = (
        P("crop", "rows", None, "hid"),
        P("crop", "rows", None, "hid"),
        P("rows", "hid", None, None),
        P("rows", "hid", None, None),
        P(None, "hid"),
        P("hid", None),
    )
    n_crop, n_rows = mesh.shape["crop"], mesh.shape["rows"]
    n_hid = mesh.shape["hid"]

    def step(tokens, cotangent, weight_in, weight_out, mix_kernel, block_rows):
        fits = (
            n_crop == 2
            and n_rows == 4
            and tokens.shape[0] == 1
            and weight_in.shape[1] % n_rows == 0
            and tokens.shape[1] * tokens.shape[2] * n_rows * tokens.shape[3] * n_hid <= 2**22
        )
        chosen = split_hidden if fits else on_device
        return chosen(tokens, cotangent, weight_in, weight_out, mix_kernel, block_rows)

    return jax.shard_map(
        step,
        mesh=mesh,
        in_specs=placed,
        out_specs=(
            P("crop", "rows", None, "hid"),
            P(("crop", "rows"), "hid", None, None),
            P(("crop", "rows"), "hid", None, None),
            P(None, "hid"),
        ),
        check_vma=False,
    )
```

```python
import functools

import jax
import jax.numpy as jnp
from jax import lax
from jax.experimental import pallas as pl
from jax.experimental.pallas import tpu as pltpu
from jax.sharding import PartitionSpec as P

root_two_pi = 0.7978845608
cubic_coef = 0.044715
loss_scale = 0.03125

MESH_ID = pl.DeviceIdType.MESH
ANY = pl.BlockSpec(memory_space=pl.ANY)
VMEM = pl.BlockSpec(memory_space=pltpu.VMEM)
SMEM = pl.BlockSpec(memory_space=pltpu.SMEM)


def span(start, size):
    return pl.ds(pl.multiple_of(start * size, size), size)


def neighbours():
    y, r, z = lax.axis_index("crop"), lax.axis_index("rows"), lax.axis_index("hid")
    x, core = r // 2, r % 2
    same_chip = x * 2 + (1 - core)
    across = (1 - x) * 2 + core
    diagonal = (1 - x) * 2 + (1 - core)
    return y, r, z, same_chip, across, diagonal


def enter(partners):
    barrier = pltpu.get_barrier_semaphore()
    for partner in partners:
        pl.semaphore_signal(barrier, inc=1, device_id=partner, device_id_type=MESH_ID)
    pl.semaphore_wait(barrier, len(partners))


def remote(src, dst, send_sem, recv_sem, target):
    return pltpu.make_async_remote_copy(
        src_ref=src,
        dst_ref=dst,
        send_sem=send_sem,
        recv_sem=recv_sem,
        device_id=target,
        device_id_type=MESH_ID,
    )


def gather_kernel(
    depth, tok, cot, w_in, w_out, tok_all, cot_all, in_all, out_all,
    raw, flat, stage, tok_send, tok_recv, w_send, w_recv, own_sem, raw_sem,
):
    y, r, z, same_chip, across, diagonal = neighbours()
    tokens, features = tok.shape
    rows = w_in.shape[0]
    lanes = in_all.shape[1]
    half = rows // 2
    block = w_in.shape[2]
    all_cols = stage.shape[1] // rows
    nnz = w_in.shape[1] // all_cols
    loads = [
        pltpu.make_async_copy(src, raw.at[a], raw_sem.at[a]) for a, src in enumerate((w_in, w_out))
    ]
    for load in loads:
        load.start()
    enter(
        [{"rows": same_chip}, {"rows": across}, {"rows": diagonal}, {"crop": 1 - y}]
        + [{"hid": (z + step) % depth} for step in range(1, depth)]
    )
    streams = ((tok, tok_all), (cot, cot_all))
    panels = ((flat.at[0], in_all), (flat.at[1], out_all))
    targets = ({"hid": z + 1}, {"hid": z - 1}, {"rows": across}, {"rows": same_chip})
    has_up, has_down = z + 1 < depth, z >= 1
    sends, local = [], []

    def launch(make, have=None):
        sends.append((make, have))
        if have is None:
            make().start()
        else:
            pl.when(have)(lambda: make().start())

    def piece(full, row, col):
        return full.at[span(row, tokens), span(col, features)]

    def pass_on(a, which, col, kind, have=None, own=False):
        def make():
            row = (r, across)[which]
            part = piece(streams[a][1], row, col)
            return remote(
                streams[a][0] if own else part,
                part,
                tok_send.at[a, which, col, kind],
                tok_recv.at[a, row, col],
                targets[kind],
            )

        launch(make, have)

    def await_piece(a, row, col, have=None):
        def wait():
            part = piece(streams[a][1], row, col)
            remote(
                part, part, tok_send.at[a, 0, 0, 3], tok_recv.at[a, row, col], {"rows": same_chip}
            ).wait_recv()

        if have is None:
            wait()
        else:
            pl.when(have)(wait)

    def half_rows(full, row, h):
        return full.at[pl.ds(pl.multiple_of(row * rows + h * half, half), half), :]

    def flatten(a):
        def turn(k, carry):
            for h in range(block // 128):
                part = raw[a, :, span(k, all_cols), h * 128 : (h + 1) * 128]
                stage[h] = part.astype(jnp.float32).reshape(rows * all_cols, 128)
            for c in range(all_cols):
                for h in range(block // 128):
                    flat[a, :, pl.ds(pl.multiple_of((c * nnz + k) * block + h * 128, 128), 128)] = stage[
                        h, pl.ds(c, rows, stride=all_cols), :
                    ].astype(jnp.bfloat16)
            return carry

        lax.fori_loop(0, nnz, turn, 0)

    def give_weights(a):
        src, full = panels[a]
        loads[a].wait()
        flatten(a)
        for slot, dest in ((1, across), (2, diagonal)):
            launch(
                lambda slot=slot, dest=dest: remote(
                    src.at[span(y, half), span(dest, lanes)],
                    half_rows(full, r, y),
                    w_send.at[a, slot],
                    w_recv.at[a, r, y],
                    {"rows": dest},
                )
            )
        launch(
            lambda: remote(
                src.at[:, span(same_chip, lanes)],
                full.at[span(r, rows), :],
                w_send.at[a, 0],
                w_recv.at[a, r, 0],
                {"rows": same_chip},
            )
        )
        keep = pltpu.make_async_copy(
            src.at[:, span(r, lanes)], full.at[span(r, rows), :], own_sem.at[a, 1]
        )
        keep.start()
        local.append(keep)

    def mirror_weights(a):
        full = panels[a][1]
        for slot, row in ((3, across), (4, diagonal)):
            part = half_rows(full, row, y)
            remote(part, part, w_send.at[a, slot], w_recv.at[a, row, y], {"rows": row}).wait_recv()
            launch(
                lambda slot=slot, row=row, part=part: remote(
                    part, part, w_send.at[a, slot], w_recv.at[a, row, y], {"crop": 1 - y}
                )
            )

    def line_step(step):
        for below in (True, False):
            col = z - step if below else z + step
            have = col >= 0 if below else col < depth
            onward = jnp.logical_and(have, has_up if below else has_down)
            for a, which in ((0, 0), (1, 0), (1, 1)):
                await_piece(a, (r, across)[which], col, have)
                pass_on(a, which, col, 0 if below else 1, onward)
                if a == 0:
                    pass_on(a, which, col, 2, have)
                pass_on(a, which, col, 3, have)

    for a, kind in ((1, 2), (0, 0), (0, 1), (1, 0), (1, 1), (0, 2), (0, 3), (1, 3)):
        pass_on(a, 0, z, kind, (has_up, has_down, None, None)[kind], own=True)
    for a in range(2):
        keep = pltpu.make_async_copy(streams[a][0], piece(streams[a][1], r, z), own_sem.at[a, 0])
        keep.start()
        local.append(keep)
    give_weights(0)
    await_piece(1, across, z)
    for kind in (0, 1, 3):
        pass_on(1, 1, z, kind, (has_up, has_down, None, None)[kind])
    give_weights(1)
    for step in range(1, depth):
        line_step(step)
        if step <= 2:
            mirror_weights(step - 1)
    for a in range(depth - 1, 2):
        mirror_weights(a)
    for step in range(depth):
        col = (z + step) % depth
        await_piece(0, across, col)
        pass_on(0, 1, col, 3)
    for a in range(2):
        full = panels[a][1]
        part = full.at[span(same_chip, rows), :]
        remote(
            part, part, w_send.at[a, 0], w_recv.at[a, same_chip, 0], {"rows": same_chip}
        ).wait_recv()
        for row in (across, diagonal):
            part = half_rows(full, row, 1 - y)
            remote(
                part, part, w_send.at[a, 0], w_recv.at[a, row, 1 - y], {"crop": 1 - y}
            ).wait_recv()
        for row in (same_chip, diagonal):
            for step in range(depth):
                await_piece(a, row, (z + step) % depth)
    for copy in local:
        copy.wait()
    for make, have in sends:
        if have is None:
            make().wait_send()
        else:
            pl.when(have)(lambda make=make: make().wait_send())


def nt(a, b):
    return lax.dot_general(a, b, (((1,), (1,)), ((), ())), preferred_element_type=jnp.float32)


def tn(a, b):
    return lax.dot_general(a, b, (((0,), (0,)), ((), ())), preferred_element_type=jnp.float32)


def local_kernel(
    width, block, cols, nnz, ids, tok, cot, w_in, w_out, taps,
    dx_out, gw_in, gw_out, kern_out, kern, dx, pre_s, act_s, slope_s, mg_s,
):
    count = tok.shape[0]
    me = lax.axis_index("rows")
    c = pl.program_id(0)
    place = lax.broadcasted_iota(jnp.int32, (count, block), 0) % width

    @pl.when(c == 0)
    def _():
        dx[...] = jnp.zeros_like(dx)
        kern[...] = jnp.zeros_like(kern)

    def spread(value):
        before = jnp.where(place == 0, 0.0, pltpu.roll(value, 1, 0))
        after = jnp.where(place == width - 1, 0.0, pltpu.roll(value, count - 1, 0))
        return (before, value, after)

    def stack_rows(up, mid, down):
        edge = jnp.zeros((width, block), jnp.float32)
        return (
            mid
            + jnp.concatenate([edge, up[:-width]], axis=0)
            + jnp.concatenate([down[width:], edge], axis=0)
        )

    hidden = span(c, block)

    def feats(k):
        return span(ids[k, me * cols + c], block)

    def panel(k):
        return slice(k * block, (k + 1) * block)

    pre = jnp.dot(tok[:, feats(0)], w_in[:, panel(0)], preferred_element_type=jnp.float32)
    for k in range(1, nnz):
        pre += jnp.dot(tok[:, feats(k)], w_in[:, panel(k)], preferred_element_type=jnp.float32)
    pre_s[...] = pre
    mg = nt(cot[:, feats(0)], w_out[:, panel(0)])
    for k in range(1, nnz):
        mg += nt(cot[:, feats(k)], w_out[:, panel(k)])
    mg_s[...] = mg.astype(jnp.bfloat16).astype(jnp.float32)
    p = pre_s[...]
    t = jnp.tanh(root_two_pi * (p + cubic_coef * p * p * p))
    act_s[...] = (0.5 * p * (1.0 + t)).astype(jnp.bfloat16).astype(jnp.float32)
    slope_s[...] = 0.5 * (1.0 + t) + 0.5 * p * (1.0 - t * t) * root_two_pi * (
        1.0 + 3.0 * cubic_coef * p * p
    )

    def tap(a, b):
        row = 3 * (a + 1) + (b + 1)
        return taps[row : row + 1, span(me * cols + c, block)]

    acts = spread(act_s[...])
    mixed = stack_rows(
        *[sum(tap(a, b) * acts[b + 1] for b in (-1, 0, 1)) for a in (-1, 0, 1)]
    ).astype(jnp.bfloat16)
    grads = mg_s[...]
    for b in (-1, 0, 1):
        seen = acts[b + 1]
        sums = (
            jnp.sum(seen[:-width] * grads[width:], axis=0, keepdims=True),
            jnp.sum(seen * grads, axis=0, keepdims=True),
            jnp.sum(seen[width:] * grads[:-width], axis=0, keepdims=True),
        )
        for a in (-1, 0, 1):
            row = 3 * (a + 1) + (b + 1)
            kern[row : row + 1, hidden] = sums[a + 1] * loss_scale
    for k in range(nnz):
        gw_out[:, panel(k)] = (tn(mixed, cot[:, feats(k)]) * loss_scale).astype(jnp.bfloat16)
    backs = spread(mg_s[...])
    gathered = stack_rows(
        *[sum(tap(a, b) * backs[1 - b] for b in (-1, 0, 1)) for a in (1, 0, -1)]
    )
    pre_grad = (gathered * slope_s[...]).astype(jnp.bfloat16)
    for k in range(nnz):
        gw_in[:, panel(k)] = (tn(tok[:, feats(k)], pre_grad) * loss_scale).astype(jnp.bfloat16)
        dx[:, feats(k)] += nt(pre_grad, w_in[:, panel(k)])

    @pl.when(c == cols - 1)
    def _():
        dx_out[...] = dx[...].astype(jnp.bfloat16)
        kern_out[...] = kern[...].astype(jnp.bfloat16)


def scatter_kernel(
    depth, dx, gw_in, gw_out, kern, dx_mine, in_mine, out_mine, kern_all,
    dx_own, gw_own, dx_near, dx_half, dx_far, dx_sum, dx_last, gw_part, gw_sum, kern_part,
    dx_send, dx_recv, gw_send, gw_recv, kern_send, kern_recv, dx_load, gw_load,
):
    y, r, z, same_chip, across, diagonal = neighbours()
    group = [same_chip, across, diagonal]
    order = (across, diagonal, same_chip, r)
    tokens, features = dx_mine.shape
    rows = in_mine.shape[0]
    lanes = gw_in.shape[1]
    weights = ((gw_in, in_mine), (gw_out, out_mine))
    enter(
        [{"rows": row} for row in group]
        + [{"crop": 1 - y}]
        + [{"hid": (z + step) % depth} for step in range(1, depth)]
    )
    started = []

    def go(*args):
        copy = remote(*args)
        copy.start()
        started.append(copy)

    go(kern, kern_part.at[1, 0], kern_send.at[0], kern_recv.at[1, 0], {"crop": 1 - y})
    for slot, row in enumerate((diagonal, same_chip)):
        go(dx.at[span(row, tokens), :], dx_near.at[slot], dx_send.at[slot], dx_recv.at[slot], {"rows": same_chip})
    for slot, row in enumerate(order):
        for a in range(2):
            go(
                weights[a][0].at[span((1 - y) * 4 + row, rows), :],
                gw_part.at[a, slot],
                gw_send.at[a, slot],
                gw_recv.at[a, slot],
                {"crop": 1 - y},
            )
    dx_loads = [
        pltpu.make_async_copy(dx.at[span(row, tokens), :], dx_own.at[slot], dx_load.at[slot])
        for slot, row in enumerate((across, r))
    ]
    gw_loads = [
        [
            pltpu.make_async_copy(
                weights[a][0].at[span(y * 4 + row, rows), :], gw_own.at[a, slot], gw_load.at[a, slot]
            )
            for a in range(2)
        ]
        for slot, row in enumerate(order)
    ]
    for load in dx_loads + [load for pair in gw_loads for load in pair]:
        load.start()
    def arrived(ref, send_sem, recv_sem, target):
        remote(ref, ref, send_sem, recv_sem, target).wait_recv()

    arrived(dx_near.at[0], dx_send.at[0], dx_recv.at[0], {"rows": same_chip})
    dx_loads[0].wait()
    dx_half[...] = (
        dx_own[0].astype(jnp.float32) + dx_near[0].astype(jnp.float32)
    ).astype(jnp.bfloat16)
    arrived(kern_part.at[1, 0], kern_send.at[0], kern_recv.at[1, 0], {"crop": 1 - y})
    kern_part[0, r] = (
        kern[...].astype(jnp.float32) + kern_part[1, 0].astype(jnp.float32)
    ).astype(jnp.bfloat16)
    for slot, row in enumerate(group):
        go(
            kern_part.at[0, r],
            kern_part.at[0, r],
            kern_send.at[slot + 1],
            kern_recv.at[0, r],
            {"rows": row},
        )
    go(dx_half, dx_far, dx_send.at[2], dx_recv.at[2], {"rows": across})
    arrived(dx_near.at[1], dx_send.at[1], dx_recv.at[1], {"rows": same_chip})
    arrived(dx_far, dx_send.at[2], dx_recv.at[2], {"rows": across})
    dx_loads[1].wait()
    for col in range(depth):
        part = slice(col * features, (col + 1) * features)
        dx_sum[col] = (
            dx_own[1, :, part].astype(jnp.float32)
            + dx_near[1, :, part].astype(jnp.float32)
            + dx_far[:, part].astype(jnp.float32)
        ).astype(jnp.bfloat16)
    for step in range(1, depth):
        go(
            dx_sum.at[(z + step) % depth],
            dx_last.at[step - 1],
            dx_send.at[2 + step],
            dx_recv.at[2 + step],
            {"hid": (z + step) % depth},
        )
    for slot, row in enumerate(order):
        for a in range(2):
            arrived(gw_part.at[a, slot], gw_send.at[a, slot], gw_recv.at[a, slot], {"crop": 1 - y})
            gw_loads[slot][a].wait()
            total = (
                gw_own[a, slot].astype(jnp.float32)
                + gw_part[a, slot].astype(jnp.float32)
            ).astype(jnp.bfloat16)
            if slot == 3:
                weights[a][1][:, span(r, lanes)] = total
            else:
                gw_sum[a, slot] = total
                go(
                    gw_sum.at[a, slot],
                    weights[a][1].at[:, span(r, lanes)],
                    gw_send.at[a, 4 + slot],
                    gw_recv.at[a, 4 + slot],
                    {"rows": row},
                )
    total = dx_sum[z].astype(jnp.float32)
    for step in range(1, depth):
        arrived(dx_last.at[step - 1], dx_send.at[2 + step], dx_recv.at[2 + step], {"hid": (z + step) % depth})
        total += dx_last[step - 1].astype(jnp.float32)
    dx_mine[...] = total.astype(jnp.bfloat16)
    for row in group:
        arrived(kern_part.at[0, row], kern_send.at[0], kern_recv.at[0, row], {"rows": same_chip})
    wide = kern.shape[1]
    for row in range(4):
        kern_all[:, row * wide : (row + 1) * wide] = kern_part[0, row].astype(jnp.float32)
    for slot, row in enumerate(order[:3]):
        for a in range(2):
            arrived(
                weights[a][1].at[:, span(row, lanes)],
                gw_send.at[a, 4 + slot],
                gw_recv.at[a, 4 + slot],
                {"rows": row},
            )
    for copy in started:
        copy.wait_send()


def finish_kernel(
    all_cols, nnz, in_mine, out_mine, dx_mine, kern_all, in_grad, out_grad, dx_grad, kern_grad
):
    block = in_grad.shape[2]
    dx_grad[...] = dx_mine[...]
    kern_grad[...] = kern_all[: kern_grad.shape[0]]
    for src, dst in ((in_mine, in_grad), (out_mine, out_grad)):
        for c in range(all_cols):
            for k in range(nnz):
                at = (c * nnz + k) * block
                dst[:, k * all_cols + c, :] = src[:, at : at + block].astype(jnp.float32)


def split_hidden(tokens, cotangent, weight_in, weight_out, mix_kernel, block_rows):
    n_rows, depth = lax.axis_size("rows"), lax.axis_size("hid")
    _, height, width, features = tokens.shape
    rows, all_cols, nnz, block = weight_in.shape
    count = height * width
    whole = count * n_rows
    model = features * depth
    cols = all_cols // n_rows
    lanes = cols * nnz * block
    hidden = cols * block
    bf16, f32 = jnp.bfloat16, jnp.float32
    dma, sds = pltpu.SemaphoreType.DMA, jax.ShapeDtypeStruct
    params = functools.partial(pltpu.CompilerParams, vmem_limit_bytes=60 * 1024 * 1024)
    tok_all, cot_all, in_all, out_all = pl.pallas_call(
        functools.partial(gather_kernel, depth),
        name="gather_parts",
        out_shape=[sds((whole, model), bf16)] * 2 + [sds((rows * n_rows, lanes), bf16)] * 2,
        in_specs=[ANY] * 4,
        out_specs=[ANY] * 4,
        scratch_shapes=[
            pltpu.VMEM((2, rows, nnz * all_cols, block), bf16),
            pltpu.VMEM((2, rows, all_cols * nnz * block), bf16),
            pltpu.VMEM((block // 128, rows * all_cols, 128), f32),
            dma((2, 2, depth, 4)),
            dma((2, n_rows, depth)),
            dma((2, 5)),
            dma((2, n_rows, 2)),
            dma((2, 2)),
            dma((2,)),
        ],
        compiler_params=params(collective_id=1, has_side_effects=True),
    )(
        tokens.reshape(count, features),
        cotangent.reshape(count, features),
        weight_in.transpose(0, 2, 1, 3).reshape(rows, nnz * all_cols, block),
        weight_out.transpose(0, 2, 1, 3).reshape(rows, nnz * all_cols, block),
    )
    panel_spec = pl.BlockSpec((block, nnz * block), lambda c: (0, c))
    dx, gw_in, gw_out, kern = pl.pallas_call(
        functools.partial(local_kernel, width, block, cols, nnz),
        name="local_math",
        out_shape=[
            sds((whole, model), bf16),
            sds((block, lanes), bf16),
            sds((block, lanes), bf16),
            sds((16, hidden), bf16),
        ],
        grid=(cols,),
        in_specs=[SMEM, VMEM, VMEM, panel_spec, panel_spec, VMEM],
        out_specs=[VMEM, panel_spec, panel_spec, VMEM],
        scratch_shapes=[pltpu.VMEM((16, hidden), f32), pltpu.VMEM((whole, model), f32)]
        + [pltpu.VMEM((whole, block), f32)] * 4,
        compiler_params=params(),
    )(block_rows.T, tok_all, cot_all, in_all, out_all, mix_kernel)
    out_rows = block // (n_rows * lax.axis_size("crop"))
    dx_mine, in_mine, out_mine, kern_all = pl.pallas_call(
        functools.partial(scatter_kernel, depth),
        name="scatter_sums",
        out_shape=[
            sds((count, features), bf16),
            sds((out_rows, all_cols * nnz * block), bf16),
            sds((out_rows, all_cols * nnz * block), bf16),
            sds((16, hidden * n_rows), f32),
        ],
        in_specs=[ANY] * 3 + [VMEM],
        out_specs=[VMEM] * 4,
        scratch_shapes=[
            pltpu.VMEM((2, count, model), bf16),
            pltpu.VMEM((2, 4, out_rows, lanes), bf16),
            pltpu.VMEM((2, count, model), bf16),
            pltpu.VMEM((count, model), bf16),
            pltpu.VMEM((count, model), bf16),
            pltpu.VMEM((depth, count, features), bf16),
            pltpu.VMEM((depth - 1, count, features), bf16),
            pltpu.VMEM((2, 4, out_rows, lanes), bf16),
            pltpu.VMEM((2, 3, out_rows, lanes), bf16),
            pltpu.VMEM((2, n_rows, 16, hidden), bf16),
            dma((2 + depth,)),
            dma((2 + depth,)),
            dma((2, 7)),
            dma((2, 7)),
            dma((4,)),
            dma((2, n_rows)),
            dma((2,)),
            dma((2, 4)),
        ],
        compiler_params=params(collective_id=2, has_side_effects=True),
    )(dx, gw_in, gw_out, kern)
    step = 8
    part = pl.BlockSpec((count * step // out_rows, features), lambda i: (i, 0))
    flat_spec = pl.BlockSpec((step, all_cols * nnz * block), lambda i: (i, 0))
    grad_spec = pl.BlockSpec((step, nnz * all_cols, block), lambda i: (i, 0, 0))
    in_grad, out_grad, dx_grad, kern_grad = pl.pallas_call(
        functools.partial(finish_kernel, all_cols, nnz),
        name="finish_weights",
        grid=(out_rows // step,),
        out_shape=[sds((out_rows, nnz * all_cols, block), f32)] * 2
        + [sds((count, features), bf16), sds(mix_kernel.shape, f32)],
        in_specs=[flat_spec] * 2 + [part, VMEM],
        out_specs=[grad_spec] * 2 + [part, VMEM],
        compiler_params=params(),
    )(in_mine, out_mine, dx_mine, kern_all)
    in_grad, out_grad = [
        grad.reshape(out_rows, nnz, all_cols, block).transpose(0, 2, 1, 3) for grad in (in_grad, out_grad)
    ]
    return (dx_grad.reshape(tokens.shape), in_grad, out_grad, kern_grad)


def padded(shard, sides, width):
    for axis, dim in sides:
        devices, length = (lax.axis_size(axis), shard.shape[dim])
        up = [(i, (i + 1) % devices) for i in range(devices - 1)]
        down = [(j, i) for i, j in up]
        last = lax.slice_in_dim(shard, length - width, length, axis=dim)
        initial = lax.slice_in_dim(shard, 0, width, axis=dim)
        before = lax.ppermute(last, axis, up)
        after = lax.ppermute(initial, axis, down)
        shard = jnp.concatenate([before, shard, after], axis=dim)
    return shard


def gelu_pair(preact):
    inner = root_two_pi * (preact + cubic_coef * preact * preact * preact)
    tanh_val = jnp.tanh(inner)
    gelu_out = 0.5 * preact * (1.0 + tanh_val)
    slopes = 0.5 * (1.0 + tanh_val) + 0.5 * preact * (1.0 - tanh_val * tanh_val) * root_two_pi * (
        1.0 + 3.0 * cubic_coef * preact * preact
    )
    return (gelu_out, slopes)


def on_device(tokens, cotangent, weight_in, weight_out, mix_kernel, block_rows):
    in_panel, out_panel = (
        lax.all_gather(weight_in, "rows", axis=0, tiled=True),
        lax.all_gather(weight_out, "rows", axis=0, tiled=True),
    )
    tok_full, cot_full = (
        lax.all_gather(tokens, "hid", axis=3, tiled=True),
        lax.all_gather(cotangent, "hid", axis=3, tiled=True),
    )
    crop_count, height, grid_width, depth_all = tok_full.shape
    tok_count = crop_count * height * grid_width
    block_size = in_panel.shape[0]
    col_count = in_panel.shape[1]
    nnz_count = in_panel.shape[2]
    block_count = depth_all // block_size
    hidden_local = col_count * block_size
    flat_rows = block_rows.reshape(-1)
    in_select = jnp.take(
        tok_full.reshape(tok_count, block_count, block_size), flat_rows, axis=1
    ).reshape(tok_count, col_count, nnz_count, block_size)
    grad_select = jnp.take(
        cot_full.reshape(tok_count, block_count, block_size), flat_rows, axis=1
    ).reshape(tok_count, col_count, nnz_count, block_size)
    pre_act = jnp.einsum("tckb,bcke->tce", in_select, in_panel, preferred_element_type=jnp.float32)
    gelu_out, slopes = gelu_pair(pre_act)
    active = gelu_out.astype(jnp.bfloat16).reshape(crop_count, height, grid_width, hidden_local)
    act_rim = padded(active, (("rows", 1),), 1)
    mix_grad = (
        jnp.einsum("tckd,fckd->tcf", grad_select, out_panel, preferred_element_type=jnp.float32)
        .astype(jnp.bfloat16)
        .reshape(crop_count, height, grid_width, hidden_local)
    )
    grad_rim = padded(mix_grad, (("rows", 1),), 1)
    act_pad = jnp.pad(act_rim.astype(jnp.float32), ((0, 0), (0, 0), (1, 1), (0, 0)))
    grad_pad = jnp.pad(grad_rim.astype(jnp.float32), ((0, 0), (0, 0), (1, 1), (0, 0)))
    grad_grid = mix_grad.astype(jnp.float32)
    mix_sum = jnp.zeros((crop_count, height, grid_width, hidden_local), jnp.float32)
    act_grad = jnp.zeros((crop_count, height, grid_width, hidden_local), jnp.float32)
    kern_terms = []
    for row_off in range(3):
        for col_off in range(3):
            tap = mix_kernel[3 * row_off + col_off]
            shifted = act_pad[:, row_off : row_off + height, col_off : col_off + grid_width]
            mix_sum = mix_sum + tap * shifted
            act_grad = (
                act_grad
                + tap
                * grad_pad[
                    :, 2 - row_off : 2 - row_off + height, 2 - col_off : 2 - col_off + grid_width
                ]
            )
            kern_terms.append(jnp.sum(shifted * grad_grid, axis=(0, 1, 2)))
    kern_local = jnp.stack(kern_terms, axis=0) * loss_scale
    mix_out = mix_sum.astype(jnp.bfloat16).reshape(tok_count, col_count, block_size)
    pre_grad = (act_grad.reshape(tok_count, col_count, block_size) * slopes).astype(jnp.bfloat16)
    kern_total = lax.psum(kern_local.astype(jnp.bfloat16), ("crop", "rows")).astype(jnp.float32)
    back_select = jnp.einsum(
        "tce,bcke->tckb", pre_grad, in_panel, preferred_element_type=jnp.float32
    )
    one_hot = (
        block_rows[:, :, None] == jnp.arange(block_count, dtype=jnp.int32)[None, None, :]
    ).astype(jnp.float32)
    token_terms = jnp.einsum(
        "tckb,ckr->trb", back_select, one_hot, precision=lax.Precision.HIGHEST
    ).reshape(crop_count, height, grid_width, depth_all)
    grad_tokens = lax.psum_scatter(
        token_terms.astype(jnp.bfloat16), "hid", scatter_dimension=3, tiled=True
    )
    first_term = jnp.einsum(
        "tckb,tce->bcke", in_select, pre_grad, preferred_element_type=jnp.float32
    )
    second_term = jnp.einsum(
        "tcf,tckd->fckd", mix_out, grad_select, preferred_element_type=jnp.float32
    )
    share_sums = lax.psum_scatter(
        (jnp.stack([first_term, second_term], axis=1) * loss_scale).astype(jnp.bfloat16),
        ("crop", "rows"),
        scatter_dimension=0,
        tiled=True,
    ).astype(jnp.float32)
    return (grad_tokens, share_sums[:, 0], share_sums[:, 1], kern_total)


def solution(mesh):
    placed = (
        P("crop", "rows", None, "hid"),
        P("crop", "rows", None, "hid"),
        P("rows", "hid", None, None),
        P("rows", "hid", None, None),
        P(None, "hid"),
        P("hid", None),
    )
    n_crop, n_rows = mesh.shape["crop"], mesh.shape["rows"]
    n_hid = mesh.shape["hid"]

    def step(tokens, cotangent, weight_in, weight_out, mix_kernel, block_rows):
        fits = (
            n_crop == 2
            and n_rows == 4
            and tokens.shape[0] == 1
            and weight_in.shape[1] % n_rows == 0
            and tokens.shape[1] * tokens.shape[2] * n_rows * tokens.shape[3] * n_hid <= 2**22
        )
        chosen = split_hidden if fits else on_device
        return chosen(tokens, cotangent, weight_in, weight_out, mix_kernel, block_rows)

    return jax.shard_map(
        step,
        mesh=mesh,
        in_specs=placed,
        out_specs=(
            P("crop", "rows", None, "hid"),
            P(("crop", "rows"), "hid", None, None),
            P(("crop", "rows"), "hid", None, None),
            P(None, "hid"),
        ),
        check_vma=False,
    )
```
